128 devices in a mesh: grp: 32 (over y, z, core), feat: 4 (over x).
Axes of the slice: x: 4, y: 4, z: 4, core: 2. Of those that a mesh axis runs over, the one named last changes fastest.
Arguments:
- hot_table: bfloat16 [16384, 1024], P(None, 'feat'), may hold values from -6 to 6
- cold_table: bfloat16 [131072, 1024], P('grp', 'feat'), may hold values from -6 to 6
- send_blocks: int32 [32, 32, 6], P('grp'), may hold values from 0 to 31
- block_counts: int32 [32, 32], P('grp'), may hold values from 1 to 6
- self_ref: int32 [90112], P('grp'), may hold values from 0 to 40959
- neigh_ref: int32 [90112, 10], P('grp'), may hold values from 0 to 40959
- route_owner: int32 [81920, 1], P('grp'), may hold values from 0 to 31; in each aligned block of 2560 rows (0 to 2559, 2560 to 5119, ...) at most 160 rows name the same one
- route_slot: int32 [81920], P('grp'), may hold values from 0 to 255
- w1_self: bfloat16 [1024, 512], P('feat'), may hold values from -0.1875 to 0.1875
- w1_neigh: bfloat16 [1024, 512], P('feat'), may hold values from -0.1875 to 0.1875
- b1_bias: float32 [512], P('feat'), may hold values from -3 to 3
- w2_self: bfloat16 [512, 512], P('feat'), may hold values from -0.25 to 0.25
- w2_neigh: bfloat16 [512, 512], P('feat'), may hold values from -0.25 to 0.25
- b2_bias: float32 [512], P('feat'), may hold values from -3 to 3
Outputs:
- embedding: bfloat16 [8192, 512], P('grp', 'feat')
The draws below stay inside these ranges and needn't reach their ends.
Inputs may be any that keep to these rules, and one draw needn't show every extreme that they name: `route_owner`: in every draw some index of grp sends exactly 160 routed rows to one owner.
All inputs are finite; a program needn't handle non-finite values.
Results may differ from the reference program's by a relative error of at most 0.0047.
Values may be sent and summed in bfloat16 or wider, within the bound.
No kernel may reach another device: no remote copies, remote signals or barrier semaphores. Data moves between devices by JAX's collectives and lax.ppermute only.
A program may use at most 192 MiB of HBM per device.

```python
import math
import jax
import jax.numpy as jnp
import numpy as np
from jax import lax

F = 1024
H = 512
BLK = 128
S1 = 10
HOT = 16384
CB_DEV = 32
NBC = 6
T2 = 256
ROUTED_DEV = 2560
L1_DEV = 2816
ROUTE_CAP = 160
COLD = 131072
TABLE = 40960
L1_ALL = 90112
ROUTED = 81920
TARGETS = 8192
N_GRP = 32


def place_ends(array, stream_key, least, top_value):
    place = [jax.random.randint(jax.random.fold_in(stream_key, axis), (), 0, length) for axis, length in enumerate(array.shape)]
    longest = array.shape.index(max(array.shape))
    beside = place[:longest] + [(place[longest] + 1) % array.shape[longest]] + place[longest + 1:]
    return array.at[tuple(place)].set(least).at[tuple(beside)].set(top_value)


def level_of(key, extent, split, low, top_value):
    level, own = 1.0, jax.random.fold_in(key, 6)
    for axis_at, parts in split:
        draws = jnp.exp(jax.random.uniform(jax.random.fold_in(own, axis_at), (parts,), jnp.float32, low / len(split), top_value / len(split)))
        level = level * jnp.repeat(draws, extent[axis_at] // parts).reshape([-1 if axis == axis_at else 1 for axis in range(len(extent))])
    return level


def shared_out(stream_key, own, number, rows, count, top, reach, lean):
    order = jax.random.permutation(stream_key, count)
    packed, usual = shares(count, rows * top, reach, lean, True), shares(count, rows * top, reach, lean, False)
    places = jnp.arange(count)

    def named(tallies, rotation):
        used = int((tallies > 0).sum())
        fixed = max(1, used // 4)
        shifted = fixed + (places - fixed + rotation * (used - fixed)) % max(1, count - fixed)
        return jnp.zeros((count,), jnp.int32).at[order[jnp.where(places < fixed, places, shifted)]].set(jnp.asarray(tallies, jnp.int32))

    tallies = jnp.where(number % 4 == 0, named(packed, number // 4), named(usual, number - number // 4 - 1))
    mixed = jax.random.permutation(jax.random.fold_in(own, 3), count)
    source_of, taker = mixed[0:count // 2 * 2:2], mixed[1:count // 2 * 2:2]
    room = jnp.minimum(tallies[source_of] - 1, reach - tallies[taker]) // 2
    room = jnp.where((source_of == order[0]) | (taker == order[0]) | (tallies[taker] == 0), 0, jnp.maximum(room, 0))
    shifted = jax.random.randint(jax.random.fold_in(own, 4), (count // 2,), 0, 1 << 20) % (room + 1)
    tallies = tallies.at[source_of].add(-shifted).at[taker].add(shifted)
    items = jnp.searchsorted(jnp.cumsum(tallies), jnp.arange(rows * top), side="right").astype(jnp.int32)
    listing = items.reshape(top, rows).T
    listing = listing[jax.random.permutation(jax.random.fold_in(own, 1), rows)]
    rotation = jax.random.randint(jax.random.fold_in(own, 2), (rows, 1), 0, top)
    return jnp.take_along_axis(listing, (jnp.arange(top)[None, :] + rotation) % top, axis=1)


def shares(amount, total, most, skew, full):
    weights = [(1 << 20) // math.isqrt(rank ** skew) + 1 for rank in range(1, amount + 1)]
    largest = most if full else min(most, max(-(-total // amount), total * weights[0] // sum(weights)))
    least = 1 if total - largest >= amount - 1 else 0
    given, spare = [largest] + [least] * (amount - 1), total - largest - least * (amount - 1)
    while spare > 0:
        candidates = [i for i in range(1, amount) if given[i] < largest] or [i for i in range(1, amount) if given[i] < most]
        mass, budget = sum([weights[i] for i in candidates]), spare
        for i in candidates:
            extra = min(most - given[i], max(1, budget * weights[i] // mass), spare)
            given[i] = given[i] + extra
            spare = spare - extra
    return np.array(given)


def centred(stream_key, shape, width, bound, shards=(), kind=jnp.bfloat16):
    entries = jax.random.normal(stream_key, shape, jnp.float32) * width
    if len(shards) > 0:
        entries = level_of(stream_key, shape, shards, -0.22, 0.18) * entries
    return jnp.clip(entries, min=-bound, max=bound).astype(kind)


def setup_inputs(seed: int = 0) -> dict:
    arg_keys = jax.random.split(jax.random.key(seed), 15)
    hot_table = centred(arg_keys[0], (HOT, F), 1.0, 6.0, ((1, 4),))
    cold_table = centred(arg_keys[1], (COLD, F), 1.0, 6.0, ((0, 32), (1, 4)))
    send_blocks = place_ends(jax.random.randint(arg_keys[2], (N_GRP, N_GRP, NBC), 0, CB_DEV), jax.random.fold_in(arg_keys[2], 1), 0, CB_DEV - 1).astype(jnp.int32)
    block_counts = place_ends(jax.random.randint(arg_keys[3], (N_GRP, N_GRP), 1, NBC + 1), jax.random.fold_in(arg_keys[3], 1), 1, NBC).astype(jnp.int32)
    self_ref = place_ends(jax.random.randint(arg_keys[4], (L1_ALL,), 0, TABLE), jax.random.fold_in(arg_keys[4], 1), 0, TABLE - 1).astype(jnp.int32)
    neigh_ref = place_ends(jax.random.randint(arg_keys[5], (L1_ALL, S1), 0, TABLE), jax.random.fold_in(arg_keys[5], 1), 0, TABLE - 1).astype(jnp.int32)
    route_owner_keys = jax.random.split(jax.random.fold_in(arg_keys[6], 1), ROUTED // ROUTED_DEV)
    route_owner_turns = jax.random.permutation(jax.random.fold_in(arg_keys[6], 3), ROUTED // ROUTED_DEV)
    route_owner = jax.vmap(lambda own, number: shared_out(jax.random.fold_in(arg_keys[6], 2), own, number, ROUTED_DEV, N_GRP, 1, ROUTE_CAP, 2))(route_owner_keys, route_owner_turns).reshape((ROUTED, 1))
    route_slot = place_ends(jax.random.randint(arg_keys[7], (ROUTED,), 0, T2), jax.random.fold_in(arg_keys[7], 1), 0, T2 - 1).astype(jnp.int32)
    w1_self = centred(arg_keys[8], (F, H), F ** -0.5, 0.1875, ((0, 4),))
    w1_neigh = centred(arg_keys[9], (F, H), F ** -0.5, 0.1875, ((0, 4),))
    b1_bias = centred(arg_keys[10], (H,), 0.5, 3.0, ((0, 4),), jnp.float32)
    w2_self = centred(arg_keys[11], (H, H), H ** -0.5, 0.25, ((0, 4),))
    w2_neigh = centred(arg_keys[12], (H, H), H ** -0.5, 0.25, ((0, 4),))
    b2_bias = centred(arg_keys[13], (H,), 0.5, 3.0, ((0, 4),), jnp.float32)
    return {"hot_table": hot_table, "cold_table": cold_table, "send_blocks": send_blocks, "block_counts": block_counts, "self_ref": self_ref, "neigh_ref": neigh_ref, "route_owner": route_owner, "route_slot": route_slot, "w1_self": w1_self, "w1_neigh": w1_neigh, "b1_bias": b1_bias, "w2_self": w2_self, "w2_neigh": w2_neigh, "b2_bias": b2_bias}


def reference(hot_table, cold_table, send_blocks, block_counts, self_ref, neigh_ref, route_owner, route_slot, w1_self, w1_neigh, b1_bias, w2_self, w2_neigh, b2_bias):
    cold_blocks = cold_table.reshape(N_GRP, CB_DEV, BLK, F)
    owners = jnp.arange(N_GRP, dtype=jnp.int32)
    slots = jnp.arange(NBC, dtype=jnp.int32)

    def layer_one(args):
        blocks, counts, selfs, neighs = args
        fetched = cold_blocks[owners[:, None], blocks]
        valid = slots[None, :] < counts[:, None]
        fetched = jnp.where(valid[:, :, None, None], fetched, jnp.zeros_like(fetched))
        table = jnp.concatenate([hot_table, fetched.reshape(-1, F)], axis=0)
        self_x = table[selfs]
        neigh_x = (jnp.sum(table[neighs], axis=1, dtype=jnp.float32) / S1).astype(jnp.bfloat16)
        pre = jnp.dot(self_x, w1_self, preferred_element_type=jnp.float32) + jnp.dot(neigh_x, w1_neigh, preferred_element_type=jnp.float32) + b1_bias
        return jnp.maximum(pre, 0.0).astype(jnp.bfloat16)

    h1 = lax.map(layer_one, (jnp.transpose(send_blocks, (1, 0, 2)), block_counts.T, self_ref.reshape(N_GRP, L1_DEV), neigh_ref.reshape(N_GRP, L1_DEV, S1)))
    own_rows = h1[:, :T2, :].reshape(TARGETS, H)
    routed = h1[:, T2:, :].reshape(ROUTED, H)
    target = route_owner[:, 0] * T2 + route_slot
    total = jax.ops.segment_sum(routed.astype(jnp.float32), target, num_segments=TARGETS)
    count = jax.ops.segment_sum(jnp.ones((ROUTED,), jnp.float32), target, num_segments=TARGETS)
    neigh_h = (total / jnp.maximum(count, 1.0)[:, None]).astype(jnp.bfloat16)
    out = jnp.dot(own_rows, w2_self, preferred_element_type=jnp.float32) + jnp.dot(neigh_h, w2_neigh, preferred_element_type=jnp.float32) + b2_bias
    return out.astype(jnp.bfloat16)
```

```python
import functools

import jax
import jax.numpy as jnp
from jax import lax
from jax.experimental import pallas as pl
from jax.experimental.pallas import tpu as pltpu
from jax.sharding import PartitionSpec as P

BLK = 128
S1 = 10
LANES = 128


def pack_kernel(blocks, counts, cold, out, zeros, sems):
    zeros[...] = jnp.zeros_like(zeros)
    total = blocks.shape[0]
    slots = total // counts.shape[0]

    def start(i, carry):
        valid = lax.rem(i, slots) < counts[i // slots]
        rows = pl.ds(pl.multiple_of(i * BLK, BLK), BLK)
        origin = pl.ds(pl.multiple_of(blocks[i] * BLK, BLK), BLK)

        @pl.when(valid)
        def _():
            pltpu.make_async_copy(cold.at[origin], out.at[rows], sems.at[i]).start()

        @pl.when(jnp.logical_not(valid))
        def _():
            pltpu.make_async_copy(zeros, out.at[rows], sems.at[i]).start()

        return carry

    def wait(i, carry):
        rows = pl.ds(pl.multiple_of(i * BLK, BLK), BLK)
        pltpu.make_async_copy(zeros, out.at[rows], sems.at[i]).wait()
        return carry

    lax.fori_loop(0, total, start, 0)
    lax.fori_loop(0, total, wait, 0)


def pack_blocks(blocks, counts, cold):
    total = blocks.shape[0]
    cols = cold.shape[1]
    return pl.pallas_call(
        pack_kernel,
        out_shape=jax.ShapeDtypeStruct((total * BLK, cols), cold.dtype),
        in_specs=[
            pl.BlockSpec(memory_space=pltpu.SMEM),
            pl.BlockSpec(memory_space=pltpu.SMEM),
            pl.BlockSpec(memory_space=pltpu.VMEM),
        ],
        out_specs=pl.BlockSpec(memory_space=pl.ANY),
        scratch_shapes=[pltpu.VMEM((BLK, cols), cold.dtype), pltpu.SemaphoreType.DMA((total,))],
        name="pack_blocks",
    )(blocks, counts, cold)


CHUNK = 1024
DEPTH = 4


def gather_kernel(index, dest, hot, fetched, out, table, stage, acc, sems):
    hot_chunks = hot.shape[0] // CHUNK
    chunks = hot_chunks + fetched.shape[0] // CHUNK
    nodes = dest.shape[0]

    def copy(c, slot):
        @pl.when(c < hot_chunks)
        def _():
            rows = pl.ds(pl.multiple_of(c * CHUNK, CHUNK), CHUNK)
            pltpu.make_async_copy(hot.at[rows], stage.at[slot], sems.at[slot]).start()

        @pl.when(c >= hot_chunks)
        def _():
            rows = pl.ds(pl.multiple_of((c - hot_chunks) * CHUNK, CHUNK), CHUNK)
            pltpu.make_async_copy(fetched.at[rows], stage.at[slot], sems.at[slot]).start()

    for c in range(DEPTH):
        copy(c, c)

    def fill(i, carry):
        acc[pl.ds(pl.multiple_of(i * 8, 8), 8), :] = jnp.zeros((8, LANES), jnp.float32)
        return carry

    lax.fori_loop(0, acc.shape[0] // 8, fill, 0, unroll=8)

    def load(c, carry):
        slot = lax.rem(c, DEPTH)
        pltpu.make_async_copy(hot.at[pl.ds(0, CHUNK)], stage.at[slot], sems.at[slot]).wait()

        def widen(g, inner):
            value = stage[slot, pl.ds(pl.multiple_of(g * 16, 16), 16), :].astype(jnp.float32)
            row = pl.multiple_of(c * (2 * CHUNK) + g * 32, 32)
            table[pl.ds(row, 16, stride=2), :] = value[:, :LANES]
            table[pl.ds(row + 1, 16, stride=2), :] = value[:, LANES:]
            return inner

        lax.fori_loop(0, CHUNK // 16, widen, 0, unroll=4)

        @pl.when(c + DEPTH < chunks)
        def _():
            copy(c + DEPTH, slot)

        return carry

    lax.fori_loop(0, chunks, load, 0)

    total = acc.shape[0] // 2

    def node(i, carry):
        place = pl.multiple_of(dest[i], 2)
        acc[pl.ds(place, 2), :] = table[pl.ds(pl.multiple_of(index[i], 2), 2), :]
        rows = [
            table[pl.ds(pl.multiple_of(index[(k + 1) * nodes + i], 2), 2), :] for k in range(S1)
        ]
        while len(rows) > 1:
            rows = [a + b for a, b in zip(rows[::2], rows[1::2])] + rows[len(rows) // 2 * 2 :]
        acc[pl.ds(total + place, 2), :] = rows[0]
        return carry

    lax.fori_loop(0, nodes, node, 0, unroll=8)

    def finish(g, carry):
        row = pl.multiple_of(g * 32, 32)
        own = [acc[pl.ds(row + j, 16, stride=2), :] for j in range(2)]
        mean = [acc[pl.ds(total + row + j, 16, stride=2), :] / S1 for j in range(2)]
        out[pl.ds(pl.multiple_of(g * 16, 16), 16), :] = jnp.concatenate(own + mean, axis=1).astype(
            jnp.bfloat16
        )
        return carry

    lax.fori_loop(0, out.shape[0] // 16, finish, 0, unroll=2)


def gather_rows(index, dest, hot, fetched, rows):
    cols = hot.shape[1]
    table_rows = hot.shape[0] + fetched.shape[0]
    return pl.pallas_call(
        gather_kernel,
        out_shape=jax.ShapeDtypeStruct((rows, 2 * cols), jnp.bfloat16),
        in_specs=[
            pl.BlockSpec(memory_space=pltpu.SMEM),
            pl.BlockSpec(memory_space=pltpu.SMEM),
            pl.BlockSpec(memory_space=pl.ANY),
            pl.BlockSpec(memory_space=pl.ANY),
        ],
        out_specs=pl.BlockSpec(memory_space=pltpu.VMEM),
        scratch_shapes=[
            pltpu.VMEM((2 * table_rows, LANES), jnp.float32),
            pltpu.VMEM((DEPTH, CHUNK, cols), jnp.bfloat16),
            pltpu.VMEM((4 * rows, LANES), jnp.float32),
            pltpu.SemaphoreType.DMA((DEPTH,)),
        ],
        compiler_params=pltpu.CompilerParams(vmem_limit_bytes=60 * 1024 * 1024),
        name="gather_rows",
    )(index, dest, hot, fetched)


def per_device(
    hot_table,
    cold_table,
    send_blocks,
    block_counts,
    self_ref,
    neigh_ref,
    route_owner,
    route_slot,
    w1_self,
    w1_neigh,
    b1_bias,
    w2_self,
    w2_neigh,
    b2_bias,
):
    groups = lax.axis_size("grp")
    parts = lax.axis_size("feat")
    me = lax.axis_index("feat")
    routed = route_slot.shape[0]
    nodes = self_ref.shape[0]
    targets = nodes - routed
    own_part = targets // parts
    hidden = w1_self.shape[1]
    hidden_part = b1_bias.shape[0]
    capacity = 2 * routed // groups
    slots = capacity // parts
    part_rows = own_part + (routed + (parts - 1) * groups) // parts
    part_rows = (part_rows + 15) // 16 * 16

    outgoing = pack_blocks(send_blocks.reshape(-1), block_counts.reshape(-1), cold_table)
    outgoing = outgoing.reshape(groups, -1, cold_table.shape[1])
    fetched = lax.all_to_all(outgoing, "grp", split_axis=0, concat_axis=0, tiled=True)
    fetched = fetched.reshape(-1, cold_table.shape[1])

    w1 = jnp.concatenate([w1_self, w1_neigh], axis=0)
    w1_all, w2s_all, b1_all = [w1], [w2_self], [b1_bias]
    for step in range(1, parts):
        ring = [(s, (s + step) % parts) for s in range(parts)]
        w1_all.append(lax.ppermute(w1, "feat", ring))
        w2s_all.append(lax.ppermute(w2_self, "feat", ring))
        b1_all.append(lax.ppermute(b1_bias, "feat", ring))
    order = lax.rem(me - jnp.arange(parts) + parts, parts)
    w1_all = jnp.stack(w1_all)[order]
    w2s_all = jnp.stack(w2s_all)[order].reshape(hidden, hidden)
    b1_all = jnp.stack(b1_all)[order].reshape(hidden)

    owner = route_owner[:, 0]
    onehot = (owner[:, None] == jnp.arange(groups, dtype=jnp.int32)[None, :]).astype(jnp.int32)
    ranks = jnp.cumsum(onehot, axis=0)
    position = jnp.sum((ranks - 1) * onehot, axis=1)
    quarter, depth = position % parts, position // parts
    totals = ranks[-1]
    held = (totals[None, :] - jnp.arange(parts)[:, None] + parts - 1) // parts
    base = jnp.cumsum(held, axis=1) - held + own_part
    owner_base = jnp.sum(onehot[:, :, None] * base.T[None, :, :], axis=1)
    mine = quarter[:, None] == jnp.arange(parts)[None, :]
    row_base = jnp.sum(jnp.where(mine, owner_base, 0), axis=1)
    routed_dest = quarter * part_rows + row_base + depth
    own = jnp.arange(targets, dtype=jnp.int32)
    own_dest = own // own_part * part_rows + own % own_part
    dest = jnp.concatenate([own_dest, routed_dest]) * 2
    index = jnp.concatenate([self_ref, neigh_ref.T.reshape(-1)]) * 2

    column = quarter * slots + depth
    named = (column[:, None] == jnp.arange(capacity, dtype=jnp.int32)[None, :]).astype(jnp.bfloat16)
    send_slots = lax.dot_general(
        onehot.astype(jnp.bfloat16),
        named * (route_slot + 1).astype(jnp.bfloat16)[:, None],
        (((0,), (0,)), ((), ())),
        preferred_element_type=jnp.float32,
    )
    send_slots = send_slots.astype(jnp.int32) - 1
    recv_slots = lax.all_to_all(send_slots, "grp", split_axis=0, concat_axis=0, tiled=True)
    recv_slots = recv_slots.reshape(groups * capacity)

    my_base = lax.dynamic_index_in_dim(base, me, 0, keepdims=False)
    my_held = lax.dynamic_index_in_dim(held, me, 0, keepdims=False)
    place = jnp.arange(slots, dtype=jnp.int32)[None, :]
    source = jnp.where(place < my_held[:, None], my_base[:, None] + place, -1).reshape(-1)
    spread = (source[:, None] == jnp.arange(part_rows, dtype=jnp.int32)[None, :]).astype(
        jnp.bfloat16
    )

    rows = gather_rows(index, dest, hot_table, fetched, parts * part_rows)
    rows = rows.reshape(parts, part_rows, -1)
    rows = lax.all_to_all(rows, "feat", split_axis=0, concat_axis=0, tiled=True)
    pre = b1_all[None, :]
    for s in range(parts):
        pre = pre + jnp.dot(rows[s], w1_all[s], preferred_element_type=jnp.float32)
    h1 = jnp.maximum(pre, 0.0).astype(jnp.bfloat16)

    send_rows = jnp.dot(spread, h1, preferred_element_type=jnp.float32).astype(jnp.bfloat16)
    send_rows = send_rows.reshape(groups, slots, parts, hidden_part).transpose(0, 2, 1, 3)
    send_rows = send_rows.reshape(groups * parts, slots, hidden_part)
    recv_rows = lax.all_to_all(send_rows, ("grp", "feat"), split_axis=0, concat_axis=0, tiled=True)
    recv_rows = recv_rows.reshape(groups * capacity, hidden_part)

    own_two = jnp.dot(h1[:own_part], w2s_all, preferred_element_type=jnp.float32)
    member = jnp.arange(targets, dtype=jnp.int32)[:, None] == recv_slots[None, :]
    total = jnp.dot(member.astype(jnp.bfloat16), recv_rows, preferred_element_type=jnp.float32)
    count = jnp.sum(member.astype(jnp.float32), axis=1)
    neigh_h = (total / jnp.maximum(count, 1.0)[:, None]).astype(jnp.bfloat16)
    partial_two = jnp.dot(neigh_h, w2_neigh, preferred_element_type=jnp.float32)
    holds = (jnp.arange(parts) == me)[:, None, None]
    partial_two = partial_two.reshape(parts, own_part, hidden) + jnp.where(holds, own_two[None], 0.0)
    partial_two = partial_two.reshape(targets, parts, hidden_part).transpose(1, 0, 2)
    shared = lax.all_to_all(partial_two, "feat", split_axis=0, concat_axis=0, tiled=True)
    return (jnp.sum(shared, axis=0) + b2_bias).astype(jnp.bfloat16)


def solution(mesh):
    in_specs = (
        P(None, "feat"),
        P("grp", "feat"),
        P("grp", None, None),
        P("grp", None),
        P("grp"),
        P("grp", None),
        P("grp", None),
        P("grp"),
        P("feat", None),
        P("feat", None),
        P("feat"),
        P("feat", None),
        P("feat", None),
        P("feat"),
    )
    out_specs = P("grp", "feat")
    return jax.shard_map(
        per_device, mesh=mesh, in_specs=in_specs, out_specs=out_specs, check_vma=False
    )
```

```python
import functools

import jax
import jax.numpy as jnp
from jax import lax
from jax.experimental import pallas as pl
from jax.experimental.pallas import tpu as pltpu
from jax.sharding import PartitionSpec as P

BLK = 128
S1 = 10
LANES = 128
HOT = 16384
MAIN = 480


def mark_kernel(refs, before, need, acc):
    owner_rows = before.shape[0]
    hot_rows = HOT
    acc[...] = jnp.zeros_like(acc)
    high = lax.broadcasted_iota(jnp.int32, (owner_rows, LANES), 0)
    low = lax.broadcasted_iota(jnp.int32, (LANES, LANES), 0)

    def count(g, carry):
        tall, wide = [], []
        for j in range(2):
            cold = refs[pl.ds(2 * g + j, 1), :] - hot_rows
            tall.append(jnp.where(high == cold >> 7, 1.0, 0.0).astype(jnp.bfloat16))
            wide.append(jnp.where(low == (cold & 127), 1.0, 0.0).astype(jnp.bfloat16))
        acc[...] += lax.dot_general(
            jnp.concatenate(tall, axis=1),
            jnp.concatenate(wide, axis=1),
            (((1,), (1,)), ((), ())),
            preferred_element_type=jnp.float32,
        )
        return carry

    lax.fori_loop(0, refs.shape[0] // 2, count, 0, unroll=11)
    needed = jnp.where(acc[...] > 0.0, 1.0, 0.0)
    upto = jnp.where(
        lax.broadcasted_iota(jnp.int32, (LANES, LANES), 0)
        <= lax.broadcasted_iota(jnp.int32, (LANES, LANES), 1),
        1.0,
        0.0,
    )
    running = jnp.dot(
        needed.astype(jnp.bfloat16), upto.astype(jnp.bfloat16), preferred_element_type=jnp.float32
    )
    totals = jnp.dot(
        needed.astype(jnp.bfloat16),
        jnp.ones((LANES, LANES), jnp.bfloat16),
        preferred_element_type=jnp.float32,
    )
    earlier = jnp.dot(before[...], totals.astype(jnp.bfloat16), preferred_element_type=jnp.float32)
    place = running + earlier - 1.0
    need[...] = jnp.where(needed > 0.0, place, -1.0).astype(jnp.int32)


def mark_rows(refs, slot_count, groups):
    rows = groups * slot_count
    at = jnp.arange(rows, dtype=jnp.int32)
    before = (at[:, None] // slot_count == at[None, :] // slot_count) & (at[None, :] < at[:, None])
    return pl.pallas_call(
        mark_kernel,
        out_shape=jax.ShapeDtypeStruct((rows, LANES), jnp.int32),
        in_specs=[pl.BlockSpec(memory_space=pltpu.VMEM)] * 2,
        out_specs=pl.BlockSpec(memory_space=pltpu.VMEM),
        scratch_shapes=[pltpu.VMEM((rows, LANES), jnp.float32)],
        name="mark_rows",
    )(refs.reshape(-1, LANES), before.astype(jnp.bfloat16))


def pack_kernel(first, slot_count, blocks, counts, need, cold, out):
    r = pl.program_id(0)
    rows = out.shape[1]
    at = lax.broadcasted_iota(jnp.int32, (rows, BLK), 0) + first
    total = jnp.zeros((rows, cold.shape[1]), jnp.float32)
    for k in range(0, slot_count, 2):
        picks, values = [], []
        for j in (k, k + 1):
            place = need[0, j : j + 1, :]
            place = jnp.where(counts[r] > j, place, -1)
            picks.append(jnp.where(at == place, 1.0, 0.0).astype(jnp.bfloat16))
            origin = pl.multiple_of(blocks[r * slot_count + j] * BLK, BLK)
            values.append(cold[pl.ds(origin, BLK), :])
        total = total + jnp.dot(
            jnp.concatenate(picks, axis=1),
            jnp.concatenate(values, axis=0),
            preferred_element_type=jnp.float32,
        )
    out[0] = total.astype(out.dtype)


def pack_needed(blocks, counts, need, cold, first, rows):
    groups = counts.shape[0]
    cols = cold.shape[1]
    return pl.pallas_call(
        functools.partial(pack_kernel, first, blocks.shape[0] // groups),
        grid=(groups,),
        out_shape=jax.ShapeDtypeStruct((groups, rows, cols), cold.dtype),
        in_specs=[
            pl.BlockSpec(memory_space=pltpu.SMEM),
            pl.BlockSpec(memory_space=pltpu.SMEM),
            pl.BlockSpec((1,) + need.shape[1:], lambda r: (r, 0, 0)),
            pl.BlockSpec(memory_space=pltpu.VMEM),
        ],
        out_specs=pl.BlockSpec((1, rows, cols), lambda r: (r, 0, 0)),
        name="pack_needed",
    )(blocks, counts, need, cold)


CHUNK = 1024
DEPTH = 4


def gather_kernel(source_count, index, where, dest, *refs):
    sources, (out, table, stage, acc, sems) = refs[:source_count], refs[source_count:]
    chunks = sum(source.shape[0] for source in sources) // CHUNK
    nodes = dest.shape[0]

    def copy(c, slot):
        begin = 0
        for source in sources:
            length = source.shape[0] // CHUNK
            first = begin

            @pl.when((c >= first) & (c < first + length))
            def _():
                rows = pl.ds(pl.multiple_of((c - first) * CHUNK, CHUNK), CHUNK)
                pltpu.make_async_copy(source.at[rows], stage.at[slot], sems.at[slot]).start()

            begin += length

    for c in range(DEPTH):
        copy(c, c)

    def fill(i, carry):
        acc[pl.ds(pl.multiple_of(i * 8, 8), 8), :] = jnp.zeros((8, LANES), jnp.float32)
        return carry

    lax.fori_loop(0, acc.shape[0] // 8, fill, 0, unroll=8)

    def load(c, carry):
        slot = lax.rem(c, DEPTH)
        pltpu.make_async_copy(sources[0].at[pl.ds(0, CHUNK)], stage.at[slot], sems.at[slot]).wait()

        def widen(g, inner):
            value = stage[slot, pl.ds(pl.multiple_of(g * 16, 16), 16), :].astype(jnp.float32)
            row = pl.multiple_of(c * (2 * CHUNK) + g * 32, 32)
            table[pl.ds(row, 16, stride=2), :] = value[:, :LANES]
            table[pl.ds(row + 1, 16, stride=2), :] = value[:, LANES:]
            return inner

        lax.fori_loop(0, CHUNK // 16, widen, 0, unroll=4)

        @pl.when(c + DEPTH < chunks)
        def _():
            copy(c + DEPTH, slot)

        return carry

    lax.fori_loop(0, chunks, load, 0)

    total = acc.shape[0] // 2

    def node(i, carry):
        place = pl.multiple_of(dest[i], 2)
        acc[pl.ds(place, 2), :] = table[pl.ds(pl.multiple_of(where[index[i]], 2), 2), :]
        rows = [
            table[pl.ds(pl.multiple_of(where[index[(k + 1) * nodes + i]], 2), 2), :] for k in range(S1)
        ]
        while len(rows) > 1:
            rows = [a + b for a, b in zip(rows[::2], rows[1::2])] + rows[len(rows) // 2 * 2 :]
        acc[pl.ds(total + place, 2), :] = rows[0]
        return carry

    lax.fori_loop(0, nodes, node, 0, unroll=8)

    def finish(g, carry):
        row = pl.multiple_of(g * 32, 32)
        own = [acc[pl.ds(row + j, 16, stride=2), :] for j in range(2)]
        mean = [acc[pl.ds(total + row + j, 16, stride=2), :] / S1 for j in range(2)]
        out[pl.ds(pl.multiple_of(g * 16, 16), 16), :] = jnp.concatenate(own + mean, axis=1).astype(
            jnp.bfloat16
        )
        return carry

    lax.fori_loop(0, out.shape[0] // 16, finish, 0, unroll=2)


def gather_rows(index, where, dest, sources, rows):
    cols = sources[0].shape[1]
    table_rows = sum(source.shape[0] for source in sources)
    return pl.pallas_call(
        functools.partial(gather_kernel, len(sources)),
        out_shape=jax.ShapeDtypeStruct((rows, 2 * cols), jnp.bfloat16),
        in_specs=[pl.BlockSpec(memory_space=pltpu.SMEM)] * 3
        + [pl.BlockSpec(memory_space=pl.ANY)] * len(sources),
        out_specs=pl.BlockSpec(memory_space=pltpu.VMEM),
        scratch_shapes=[
            pltpu.VMEM((2 * table_rows, LANES), jnp.float32),
            pltpu.VMEM((DEPTH, CHUNK, cols), jnp.bfloat16),
            pltpu.VMEM((4 * rows, LANES), jnp.float32),
            pltpu.SemaphoreType.DMA((DEPTH,)),
        ],
        compiler_params=pltpu.CompilerParams(vmem_limit_bytes=60 * 1024 * 1024),
        name="gather_rows",
    )(index, where, dest, *sources)


def per_device(
    hot_table,
    cold_table,
    send_blocks,
    block_counts,
    self_ref,
    neigh_ref,
    route_owner,
    route_slot,
    w1_self,
    w1_neigh,
    b1_bias,
    w2_self,
    w2_neigh,
    b2_bias,
):
    groups = lax.axis_size("grp")
    parts = lax.axis_size("feat")
    me = lax.axis_index("feat")
    routed = route_slot.shape[0]
    nodes = self_ref.shape[0]
    targets = nodes - routed
    own_part = targets // parts
    hidden = w1_self.shape[1]
    hidden_part = b1_bias.shape[0]
    capacity = 2 * routed // groups
    slots = capacity // parts
    part_rows = own_part + (routed + (parts - 1) * groups) // parts
    part_rows = (part_rows + 15) // 16 * 16

    feat_cols = cold_table.shape[1]
    slot_count = send_blocks.shape[2]
    fetch_rows = slot_count * BLK
    index = jnp.concatenate([self_ref, neigh_ref.T.reshape(-1)])
    need = mark_rows(index, slot_count, groups).reshape(groups, fetch_rows)
    spills = (jnp.max(need) >= MAIN).astype(jnp.int32)

    w1 = jnp.concatenate([w1_self, w1_neigh], axis=0)
    w1_all, w2s_all, b1_all = [w1], [w2_self], [b1_bias]
    for step in range(1, parts):
        ring = [(s, (s + step) % parts) for s in range(parts)]
        w1_all.append(lax.ppermute(w1, "feat", ring))
        w2s_all.append(lax.ppermute(w2_self, "feat", ring))
        b1_all.append(lax.ppermute(b1_bias, "feat", ring))
    order = lax.rem(me - jnp.arange(parts) + parts, parts)
    w1_all = jnp.stack(w1_all)[order]
    w2s_all = jnp.stack(w2s_all)[order].reshape(hidden, hidden)
    b1_all = jnp.stack(b1_all)[order].reshape(hidden)

    owner = route_owner[:, 0]
    onehot = (owner[:, None] == jnp.arange(groups, dtype=jnp.int32)[None, :]).astype(jnp.int32)
    spans = routed // LANES
    upto = jnp.arange(LANES)[:, None] <= jnp.arange(LANES)[None, :]
    running = jnp.dot(
        onehot.T.astype(jnp.bfloat16).reshape(groups * spans, LANES),
        upto.astype(jnp.bfloat16),
        preferred_element_type=jnp.float32,
    ).reshape(groups, spans, LANES)
    span_totals = running[:, :, -1]
    before = jnp.arange(spans)[:, None] < jnp.arange(spans)[None, :]
    earlier = jnp.dot(
        span_totals.astype(jnp.bfloat16), before.astype(jnp.bfloat16), preferred_element_type=jnp.float32
    )
    ranks = (running + earlier[:, :, None]).astype(jnp.int32).reshape(groups, routed)
    position = jnp.sum((ranks - 1) * onehot.T, axis=0)
    quarter, depth = position % parts, position // parts
    totals = ranks[:, -1]
    held = (totals[None, :] - jnp.arange(parts)[:, None] + parts - 1) // parts
    base = jnp.cumsum(held, axis=1) - held + own_part
    owner_base = jnp.sum(onehot[:, :, None] * base.T[None, :, :], axis=1)
    mine = quarter[:, None] == jnp.arange(parts)[None, :]
    row_base = jnp.sum(jnp.where(mine, owner_base, 0), axis=1)
    routed_dest = quarter * part_rows + row_base + depth
    own = jnp.arange(targets, dtype=jnp.int32)
    own_dest = own // own_part * part_rows + own % own_part
    dest = jnp.concatenate([own_dest, routed_dest]) * 2

    column = quarter * slots + depth
    named = (column[:, None] == jnp.arange(capacity, dtype=jnp.int32)[None, :]).astype(jnp.bfloat16)
    send_slots = lax.dot_general(
        onehot.astype(jnp.bfloat16),
        named * (route_slot + 1).astype(jnp.bfloat16)[:, None],
        (((0,), (0,)), ((), ())),
        preferred_element_type=jnp.float32,
    )
    send_slots = send_slots.astype(jnp.int32) - 1
    flags = jnp.broadcast_to(spills, (groups, LANES - capacity % LANES))
    notes = jnp.concatenate([need, send_slots, flags], axis=1)
    notes = lax.all_to_all(notes, "grp", split_axis=0, concat_axis=0, tiled=True)
    recv_slots = notes[:, fetch_rows : fetch_rows + capacity].reshape(groups * capacity)
    spilled = jnp.max(notes[:, fetch_rows + capacity]) > 0

    owner_at = jnp.arange(groups, dtype=jnp.int32)[:, None]
    spill = fetch_rows - MAIN
    where = jnp.where(
        need < MAIN,
        HOT + owner_at * MAIN + need,
        HOT + groups * MAIN + owner_at * spill + need - MAIN,
    )
    where = jnp.concatenate([jnp.arange(HOT, dtype=jnp.int32), where.reshape(-1)]) * 2

    def exchange(first, rows, prepared):
        outgoing = pack_needed(
            send_blocks.reshape(-1),
            block_counts.reshape(-1),
            notes.reshape(groups, -1, LANES),
            cold_table,
            first,
            rows,
        )
        outgoing, prepared = lax.optimization_barrier((outgoing, prepared))
        fetched = lax.all_to_all(outgoing, "grp", split_axis=0, concat_axis=0, tiled=True)
        fetched, prepared = lax.optimization_barrier((fetched, prepared))
        return fetched.reshape(-1, feat_cols), prepared

    my_base = lax.dynamic_index_in_dim(base, me, 0, keepdims=False)
    my_held = lax.dynamic_index_in_dim(held, me, 0, keepdims=False)
    place = jnp.arange(slots, dtype=jnp.int32)[None, :]
    source = jnp.where(place < my_held[:, None], my_base[:, None] + place, -1).reshape(-1)
    spread = (source[:, None] == jnp.arange(part_rows, dtype=jnp.int32)[None, :]).astype(
        jnp.bfloat16
    )

    prepared = (w1_all, w2s_all, b1_all, index, where, dest, recv_slots, spread, spilled)
    main, prepared = exchange(0, MAIN, prepared)
    w1_all, w2s_all, b1_all, index, where, dest, recv_slots, spread, spilled = prepared

    def with_spill():
        extra, _ = exchange(MAIN, spill, ())
        return gather_rows(index, where, dest, [hot_table, main, extra], parts * part_rows)

    def without_spill():
        return gather_rows(index, where, dest, [hot_table, main], parts * part_rows)

    rows = lax.cond(spilled, with_spill, without_spill)
    rows = rows.reshape(parts, part_rows, -1)
    rows = lax.all_to_all(rows, "feat", split_axis=0, concat_axis=0, tiled=True)
    pre = b1_all[None, :]
    for s in range(parts):
        pre = pre + jnp.dot(rows[s], w1_all[s], preferred_element_type=jnp.float32)
    h1 = jnp.maximum(pre, 0.0).astype(jnp.bfloat16)

    send_rows = jnp.dot(spread, h1, preferred_element_type=jnp.float32).astype(jnp.bfloat16)
    send_rows = send_rows.reshape(groups, slots, parts, hidden_part).transpose(0, 2, 1, 3)
    send_rows = send_rows.reshape(groups * parts, slots, hidden_part)
    recv_rows = lax.all_to_all(send_rows, ("grp", "feat"), split_axis=0, concat_axis=0, tiled=True)
    recv_rows = recv_rows.reshape(groups * capacity, hidden_part)

    own_two = jnp.dot(h1[:own_part], w2s_all, preferred_element_type=jnp.float32)
    member = jnp.arange(targets, dtype=jnp.int32)[:, None] == recv_slots[None, :]
    total = jnp.dot(member.astype(jnp.bfloat16), recv_rows, preferred_element_type=jnp.float32)
    count = jnp.sum(member.astype(jnp.float32), axis=1)
    neigh_h = (total / jnp.maximum(count, 1.0)[:, None]).astype(jnp.bfloat16)
    partial_two = jnp.dot(neigh_h, w2_neigh, preferred_element_type=jnp.float32)
    holds = (jnp.arange(parts) == me)[:, None, None]
    partial_two = partial_two.reshape(parts, own_part, hidden) + jnp.where(holds, own_two[None], 0.0)
    partial_two = partial_two.reshape(targets, parts, hidden_part).transpose(1, 0, 2)
    shared = lax.all_to_all(partial_two, "feat", split_axis=0, concat_axis=0, tiled=True)
    return (jnp.sum(shared, axis=0) + b2_bias).astype(jnp.bfloat16)


def solution(mesh):
    in_specs = (
        P(None, "feat"),
        P("grp", "feat"),
        P("grp", None, None),
        P("grp", None),
        P("grp"),
        P("grp", None),
        P("grp", None),
        P("grp"),
        P("feat", None),
        P("feat", None),
        P("feat"),
        P("feat", None),
        P("feat", None),
        P("feat"),
    )
    out_specs = P("grp", "feat")
    return jax.shard_map(
        per_device, mesh=mesh, in_specs=in_specs, out_specs=out_specs, check_vma=False
    )
```

```python
import functools

import jax
import jax.numpy as jnp
from jax import lax
from jax.experimental import pallas as pl
from jax.experimental.pallas import tpu as pltpu
from jax.sharding import PartitionSpec as P

BLK = 128
S1 = 10
LANES = 128
HOT = 16384
MAIN = 480
PREFIX_AT = 32
FLAG_AT = 64


def mark_kernel(refs, before, owners, extras, notes, look, acc):
    owner_rows = before.shape[0]
    groups = notes.shape[0]
    slot_count = owner_rows // groups
    acc[...] = jnp.zeros_like(acc)
    high = lax.broadcasted_iota(jnp.int32, (owner_rows, LANES), 0)
    low = lax.broadcasted_iota(jnp.int32, (LANES, LANES), 0)

    def count(g, carry):
        tall, wide = [], []
        for j in range(2):
            cold = refs[pl.ds(2 * g + j, 1), :] - HOT
            tall.append(jnp.where(high == cold >> 7, 1.0, 0.0).astype(jnp.bfloat16))
            wide.append(jnp.where(low == (cold & 127), 1.0, 0.0).astype(jnp.bfloat16))
        acc[...] += lax.dot_general(
            jnp.concatenate(tall, axis=1),
            jnp.concatenate(wide, axis=1),
            (((1,), (1,)), ((), ())),
            preferred_element_type=jnp.float32,
        )
        return carry

    lax.fori_loop(0, refs.shape[0] // 2, count, 0, unroll=11)
    needed = jnp.where(acc[...] > 0.0, 1.0, 0.0)
    upto = jnp.where(low <= lax.broadcasted_iota(jnp.int32, (LANES, LANES), 1), 1.0, 0.0)
    running = jnp.dot(
        needed.astype(jnp.bfloat16), upto.astype(jnp.bfloat16), preferred_element_type=jnp.float32
    )
    totals = jnp.dot(
        needed.astype(jnp.bfloat16),
        jnp.ones((LANES, LANES), jnp.bfloat16),
        preferred_element_type=jnp.float32,
    )
    earlier = jnp.dot(before[...], totals.astype(jnp.bfloat16), preferred_element_type=jnp.float32)
    local = jnp.where(needed > 0.0, running - 1.0, -1.0)
    place = jnp.where(needed > 0.0, earlier + running - 1.0, -1.0)
    spills = jnp.where(jnp.max(place) >= MAIN, 1, 0)
    place = place.astype(jnp.int32)
    lane = lax.broadcasted_iota(jnp.int32, (slot_count, LANES), 1)
    slot_lane = lane - PREFIX_AT == lax.broadcasted_iota(jnp.int32, (slot_count, LANES), 0)
    row_lane = lax.broadcasted_iota(jnp.int32, (1, LANES), 1)
    for o in range(groups):
        span = slice(o * slot_count, (o + 1) * slot_count)
        notes[o, 0:slot_count, :] = place[span]
        prefix = jnp.sum(jnp.where(slot_lane, earlier[span], 0.0), axis=0, keepdims=True)
        last = jnp.where(row_lane < PREFIX_AT, extras[o, 1:2, :], prefix.astype(jnp.int32))
        notes[o, slot_count : slot_count + 1, :] = extras[o, 0:1, :]
        notes[o, slot_count + 1 : slot_count + 2, :] = jnp.where(row_lane >= FLAG_AT, spills, last)
    across = jnp.transpose(earlier)[0:1]
    eighth = jnp.floor(across * 0.125)
    rest = jnp.zeros((5, owner_rows), jnp.float32)
    rows = [jnp.transpose(local), owners[0:1, :], eighth, across - 8.0 * eighth, rest]
    look[...] = jnp.concatenate(rows, axis=0).astype(jnp.bfloat16)


def mark_rows(refs, extras, slot_count, groups):
    rows = groups * slot_count
    at = jnp.arange(rows, dtype=jnp.int32)
    before = (at[:, None] // slot_count == at[None, :] // slot_count) & (at[None, :] < at[:, None])
    owners = jnp.broadcast_to((at // slot_count).astype(jnp.float32)[None, :], (8, rows))
    return pl.pallas_call(
        mark_kernel,
        out_shape=(
            jax.ShapeDtypeStruct((groups, slot_count + 2, LANES), jnp.int32),
            jax.ShapeDtypeStruct((LANES + 8, rows), jnp.bfloat16),
        ),
        in_specs=[pl.BlockSpec(memory_space=pltpu.VMEM)] * 4,
        out_specs=(pl.BlockSpec(memory_space=pltpu.VMEM),) * 2,
        scratch_shapes=[pltpu.VMEM((rows, LANES), jnp.float32)],
        name="mark_rows",
    )(refs, before.astype(jnp.bfloat16), owners, extras)


def remap_kernel(spill, groups, refs, look, *outs):
    owner_rows = look.shape[1]
    high = lax.broadcasted_iota(jnp.int32, (owner_rows, LANES), 0)
    low = lax.broadcasted_iota(jnp.int32, (LANES, LANES), 0)
    rows = outs[0].shape[0]
    table = look[...]
    for k, out in enumerate(outs):

        def lookup(g, carry, k=k, out=out):
            names = [refs[pl.ds(k * rows + 2 * g + j, 1), :] for j in range(2)]
            tall = [
                jnp.where(high == (name - HOT) >> 7, 1.0, 0.0).astype(jnp.bfloat16)
                for name in names
            ]
            found = jnp.dot(
                table, jnp.concatenate(tall, axis=1), preferred_element_type=jnp.float32
            )
            for j, name in enumerate(names):
                part = found[:, j * LANES : (j + 1) * LANES]
                local = jnp.where(low == ((name - HOT) & 127), part[:LANES], 0.0)
                local = jnp.sum(local, axis=0, keepdims=True)
                owner, eighth, unit = (part[LANES + n : LANES + n + 1] for n in range(3))
                place = 8.0 * eighth + unit + local
                cold = jnp.where(
                    place < MAIN,
                    HOT + owner * MAIN + place,
                    HOT + groups * MAIN + owner * spill + place - MAIN,
                ).astype(jnp.int32)
                out[pl.ds(2 * g + j, 1), :] = jnp.where(name < HOT, name, cold) * 2
            return carry

        lax.fori_loop(0, rows // 2, lookup, 0, unroll=11)


def remap(refs, look, nodes, spill, groups):
    count = refs.shape[0] * LANES // nodes
    outs = pl.pallas_call(
        functools.partial(remap_kernel, spill, groups),
        out_shape=[jax.ShapeDtypeStruct((nodes // LANES, LANES), jnp.int32)] * count,
        in_specs=[pl.BlockSpec(memory_space=pltpu.VMEM)] * 2,
        out_specs=[pl.BlockSpec(memory_space=pltpu.VMEM)] * count,
        name="remap",
    )(refs, look)
    return tuple(out.reshape(nodes) for out in outs)


def pack_kernel(first, slot_count, blocks, counts, prefix, need, cold, out, left, right):
    r = pl.program_id(0)
    rows = out.shape[1]
    at = lax.broadcasted_iota(jnp.int32, (BLK, BLK), 0)
    for k in range(slot_count):
        begin = prefix[r * slot_count + k]
        place = need[0, k : k + 1, :] - begin
        place = jnp.where(counts[r] > k, place, -1)
        picks = jnp.where(at == place, 1.0, 0.0).astype(jnp.bfloat16)
        origin = pl.multiple_of(blocks[r * slot_count + k] * BLK, BLK)
        value = jnp.dot(picks, cold[pl.ds(origin, BLK), :], preferred_element_type=jnp.float32)
        left[pl.ds(begin, BLK), :] = value[:, :LANES]
        right[pl.ds(begin, BLK), :] = value[:, LANES:]
    out[0, :, :LANES] = left[first : first + rows, :].astype(out.dtype)
    out[0, :, LANES:] = right[first : first + rows, :].astype(out.dtype)


def pack_needed(blocks, counts, prefix, need, cold, first, rows):
    groups = counts.shape[0]
    cols = cold.shape[1]
    slot_count = blocks.shape[0] // groups
    return pl.pallas_call(
        functools.partial(pack_kernel, first, slot_count),
        grid=(groups,),
        out_shape=jax.ShapeDtypeStruct((groups, rows, cols), cold.dtype),
        in_specs=[
            pl.BlockSpec(memory_space=pltpu.SMEM),
            pl.BlockSpec(memory_space=pltpu.SMEM),
            pl.BlockSpec(memory_space=pltpu.SMEM),
            pl.BlockSpec((1,) + need.shape[1:], lambda r: (r, 0, 0)),
            pl.BlockSpec(memory_space=pltpu.VMEM),
        ],
        out_specs=pl.BlockSpec((1, rows, cols), lambda r: (r, 0, 0)),
        scratch_shapes=[pltpu.VMEM((slot_count * BLK + BLK, LANES), jnp.float32)] * 2,
        name="pack_needed",
    )(blocks, counts, prefix, need, cold)


def layer_one_kernel(me, base, rows, *refs):
    weights, (out, own_two, hidden, bias) = refs[:-4], refs[-4:]
    parts = len(weights)
    depth = rows.shape[2]
    width = weights[0].shape[1]
    groups, _, slots, cols = out.shape
    own_part = own_two.shape[0]
    total_rows = rows.shape[1]
    sources = [lax.rem(me[0] - step + parts, parts) for step in range(parts)]
    for source, weight in zip(sources, weights):
        tail = weight[depth + cols : depth + cols + 8, :cols].astype(jnp.float32)
        bias[:, pl.ds(pl.multiple_of(source * cols, cols), cols)] = (
            tail[0:1] + tail[1:2] + tail[2:3]
        )
    chunk = total_rows // 4
    for c in range(4):
        span = slice(c * chunk, (c + 1) * chunk)
        pre = jnp.broadcast_to(bias[...], (chunk, width))
        for source, weight in zip(sources, weights):
            pre = pre + jnp.dot(
                rows[source, span, :], weight[0:depth, :], preferred_element_type=jnp.float32
            )
        h1 = jnp.maximum(pre, 0.0).astype(jnp.bfloat16).astype(jnp.float32)
        for f in range(parts):
            hidden[f, span, :] = h1[:, f * cols : (f + 1) * cols]
    for f in range(parts):
        hidden[f, total_rows:, :] = jnp.zeros((hidden.shape[1] - total_rows, cols), jnp.float32)
    total = jnp.zeros((own_part, width), jnp.float32)
    for source, weight in zip(sources, weights):
        total = total + jnp.dot(
            hidden[source, 0:own_part, :].astype(jnp.bfloat16),
            weight[depth : depth + cols, :],
            preferred_element_type=jnp.float32,
        )
    own_two[...] = total

    def send(o, carry):
        for f in range(parts):
            out[o, f] = hidden[f, pl.ds(base[o], slots), :].astype(out.dtype)
        return carry

    lax.fori_loop(0, groups, send, 0)


def layer_one(me, base, rows, weights, groups, slots, own_part):
    parts, total_rows, _ = rows.shape
    width = weights[0].shape[1]
    cols = width // parts
    return pl.pallas_call(
        layer_one_kernel,
        out_shape=(
            jax.ShapeDtypeStruct((groups, parts, slots, cols), jnp.bfloat16),
            jax.ShapeDtypeStruct((own_part, width), jnp.float32),
        ),
        in_specs=[pl.BlockSpec(memory_space=pltpu.SMEM)] * 2
        + [pl.BlockSpec(memory_space=pltpu.VMEM)] * (1 + len(weights)),
        out_specs=(pl.BlockSpec(memory_space=pltpu.VMEM),) * 2,
        scratch_shapes=[
            pltpu.VMEM((parts, total_rows + slots, cols), jnp.float32),
            pltpu.VMEM((1, width), jnp.float32),
        ],
        name="layer_one",
    )(me, base, rows, *weights)


CHUNK = 1024
DEPTH = 4


def gather_kernel(source_count, dest, *refs):
    index, refs = refs[: S1 + 1], refs[S1 + 1 :]
    sources, (out, table, stage, acc, sems) = refs[:source_count], refs[source_count:]
    chunks = sum(source.shape[0] for source in sources) // CHUNK
    nodes = dest.shape[0]

    def copy(c, slot):
        begin = 0
        for source in sources:
            length = source.shape[0] // CHUNK
            first = begin

            @pl.when((c >= first) & (c < first + length))
            def _():
                rows = pl.ds(pl.multiple_of((c - first) * CHUNK, CHUNK), CHUNK)
                pltpu.make_async_copy(source.at[rows], stage.at[slot], sems.at[slot]).start()

            begin += length

    for c in range(DEPTH):
        copy(c, c)

    def fill(i, carry):
        acc[pl.ds(pl.multiple_of(i * 8, 8), 8), :] = jnp.zeros((8, LANES), jnp.float32)
        return carry

    lax.fori_loop(0, acc.shape[0] // 8, fill, 0, unroll=8)

    def load(c, carry):
        slot = lax.rem(c, DEPTH)
        pltpu.make_async_copy(sources[0].at[pl.ds(0, CHUNK)], stage.at[slot], sems.at[slot]).wait()

        def widen(g, inner):
            value = stage[slot, pl.ds(pl.multiple_of(g * 16, 16), 16), :].astype(jnp.float32)
            row = pl.multiple_of(c * (2 * CHUNK) + g * 32, 32)
            table[pl.ds(row, 16, stride=2), :] = value[:, :LANES]
            table[pl.ds(row + 1, 16, stride=2), :] = value[:, LANES:]
            return inner

        lax.fori_loop(0, CHUNK // 16, widen, 0, unroll=4)

        @pl.when(c + DEPTH < chunks)
        def _():
            copy(c + DEPTH, slot)

        return carry

    lax.fori_loop(0, chunks, load, 0)

    total = acc.shape[0] // 2

    def node(i, carry):
        place = pl.multiple_of(dest[i], 2)
        acc[pl.ds(place, 2), :] = table[pl.ds(pl.multiple_of(index[0][i], 2), 2), :]
        rows = [
            table[pl.ds(pl.multiple_of(index[k + 1][i], 2), 2), :] for k in range(S1)
        ]
        while len(rows) > 1:
            rows = [a + b for a, b in zip(rows[::2], rows[1::2])] + rows[len(rows) // 2 * 2 :]
        acc[pl.ds(total + place, 2), :] = rows[0]
        return carry

    lax.fori_loop(0, nodes, node, 0, unroll=8)

    def finish(g, carry):
        row = pl.multiple_of(g * 32, 32)
        own = [acc[pl.ds(row + j, 16, stride=2), :] for j in range(2)]
        mean = [acc[pl.ds(total + row + j, 16, stride=2), :] / S1 for j in range(2)]
        out[pl.ds(pl.multiple_of(g * 16, 16), 16), :] = jnp.concatenate(own + mean, axis=1).astype(
            jnp.bfloat16
        )
        return carry

    lax.fori_loop(0, out.shape[0] // 16, finish, 0, unroll=2)


def gather_rows(index, dest, sources, rows):
    cols = sources[0].shape[1]
    table_rows = sum(source.shape[0] for source in sources)
    return pl.pallas_call(
        functools.partial(gather_kernel, len(sources)),
        out_shape=jax.ShapeDtypeStruct((rows, 2 * cols), jnp.bfloat16),
        in_specs=[pl.BlockSpec(memory_space=pltpu.SMEM)] * (1 + len(index))
        + [pl.BlockSpec(memory_space=pl.ANY)] * len(sources),
        out_specs=pl.BlockSpec(memory_space=pltpu.VMEM),
        scratch_shapes=[
            pltpu.VMEM((2 * table_rows, LANES), jnp.float32),
            pltpu.VMEM((DEPTH, CHUNK, cols), jnp.bfloat16),
            pltpu.VMEM((4 * rows, LANES), jnp.float32),
            pltpu.SemaphoreType.DMA((DEPTH,)),
        ],
        compiler_params=pltpu.CompilerParams(vmem_limit_bytes=60 * 1024 * 1024),
        name="gather_rows",
    )(dest, *index, *sources)


def per_device(
    hot_table,
    cold_table,
    send_blocks,
    block_counts,
    self_ref,
    neigh_ref,
    route_owner,
    route_slot,
    w1_self,
    w1_neigh,
    b1_bias,
    w2_self,
    w2_neigh,
    b2_bias,
):
    groups = lax.axis_size("grp")
    parts = lax.axis_size("feat")
    me = lax.axis_index("feat")
    routed = route_slot.shape[0]
    nodes = self_ref.shape[0]
    targets = nodes - routed
    own_part = targets // parts
    hidden = w1_self.shape[1]
    hidden_part = b1_bias.shape[0]
    capacity = 2 * routed // groups
    slots = capacity // parts
    part_rows = own_part + (routed + (parts - 1) * groups) // parts
    part_rows = (part_rows + 15) // 16 * 16

    feat_cols = cold_table.shape[1]
    slot_count = send_blocks.shape[2]
    fetch_rows = slot_count * BLK
    refs = jnp.concatenate([self_ref, neigh_ref.T.reshape(-1)]).reshape(-1, LANES)

    coarse = lax.reduce_precision(b1_bias, 8, 7)
    middle = lax.reduce_precision(b1_bias - coarse, 8, 7)
    fine = b1_bias - coarse - middle
    bias_rows = jnp.stack([coarse, middle, fine]).astype(jnp.bfloat16)
    bias_rows = jnp.pad(bias_rows, ((0, 16 - 3), (0, hidden - hidden_part)))
    weight = jnp.concatenate([w1_self, w1_neigh, w2_self, bias_rows], axis=0)
    weights = [weight]
    for step in range(1, parts):
        ring = [(s, (s + step) % parts) for s in range(parts)]
        weights.append(lax.ppermute(weight, "feat", ring))

    owner = route_owner[:, 0]
    onehot = (owner[:, None] == jnp.arange(groups, dtype=jnp.int32)[None, :]).astype(jnp.int32)
    spans = routed // LANES
    upto = jnp.arange(LANES)[:, None] <= jnp.arange(LANES)[None, :]
    running = jnp.dot(
        onehot.T.astype(jnp.bfloat16).reshape(groups * spans, LANES),
        upto.astype(jnp.bfloat16),
        preferred_element_type=jnp.float32,
    ).reshape(groups, spans, LANES)
    span_totals = running[:, :, -1]
    before = jnp.arange(spans)[:, None] < jnp.arange(spans)[None, :]
    earlier = jnp.dot(
        span_totals.astype(jnp.bfloat16), before.astype(jnp.bfloat16), preferred_element_type=jnp.float32
    )
    ranks = (running + earlier[:, :, None]).astype(jnp.int32).reshape(groups, routed)
    position = jnp.sum((ranks - 1) * onehot.T, axis=0)
    quarter, depth = position % parts, position // parts
    totals = ranks[:, -1]
    held = (totals[None, :] - jnp.arange(parts)[:, None] + parts - 1) // parts
    base = jnp.cumsum(held, axis=1) - held + own_part
    owner_base = jnp.sum(onehot[:, :, None] * base.T[None, :, :], axis=1)
    mine = quarter[:, None] == jnp.arange(parts)[None, :]
    row_base = jnp.sum(jnp.where(mine, owner_base, 0), axis=1)
    routed_dest = quarter * part_rows + row_base + depth
    own = jnp.arange(targets, dtype=jnp.int32)
    own_dest = own // own_part * part_rows + own % own_part
    dest = jnp.concatenate([own_dest, routed_dest]) * 2

    column = quarter * slots + depth
    named = (column[:, None] == jnp.arange(capacity, dtype=jnp.int32)[None, :]).astype(jnp.bfloat16)
    send_slots = lax.dot_general(
        onehot.astype(jnp.bfloat16),
        named * (route_slot + 1).astype(jnp.bfloat16)[:, None],
        (((0,), (0,)), ((), ())),
        preferred_element_type=jnp.float32,
    )
    send_slots = send_slots.astype(jnp.int32) - 1
    extras = jnp.pad(send_slots, ((0, 0), (0, 2 * LANES - capacity))).reshape(groups, 2, LANES)
    notes, look = mark_rows(refs, extras, slot_count, groups)
    notes = lax.all_to_all(notes, "grp", split_axis=0, concat_axis=0, tiled=True)
    spill = fetch_rows - MAIN
    index = remap(refs, look, nodes, spill, groups)
    recv_slots = notes[:, slot_count:, :].reshape(groups, -1)[:, :capacity]
    recv_slots = recv_slots.reshape(groups * capacity)
    spilled = jnp.max(notes[:, slot_count + 1, FLAG_AT]) > 0
    prefix = notes[:, slot_count + 1, PREFIX_AT : PREFIX_AT + slot_count].reshape(-1)

    def exchange(first, rows, prepared):
        outgoing = pack_needed(
            send_blocks.reshape(-1),
            block_counts.reshape(-1),
            prefix,
            notes,
            cold_table,
            first,
            rows,
        )
        outgoing, prepared = lax.optimization_barrier((outgoing, prepared))
        fetched = lax.all_to_all(outgoing, "grp", split_axis=0, concat_axis=0, tiled=True)
        fetched, prepared = lax.optimization_barrier((fetched, prepared))
        return fetched.reshape(-1, feat_cols), prepared

    my_base = lax.dynamic_index_in_dim(base, me, 0, keepdims=False)

    prepared = (weights, index, dest, recv_slots, my_base, spilled)
    main, prepared = exchange(0, MAIN, prepared)
    weights, index, dest, recv_slots, my_base, spilled = prepared

    def with_spill():
        extra, _ = exchange(MAIN, spill, ())
        return gather_rows(index, dest, [hot_table, main, extra], parts * part_rows)

    def without_spill():
        return gather_rows(index, dest, [hot_table, main], parts * part_rows)

    rows = lax.cond(spilled, with_spill, without_spill)
    rows = rows.reshape(parts, part_rows, -1)
    rows = lax.all_to_all(rows, "feat", split_axis=0, concat_axis=0, tiled=True)
    send_rows, own_two = layer_one(
        me.reshape(1), my_base, rows, weights, groups, slots, own_part
    )
    send_rows = send_rows.reshape(groups * parts, slots, hidden_part)
    recv_rows = lax.all_to_all(send_rows, ("grp", "feat"), split_axis=0, concat_axis=0, tiled=True)
    recv_rows = recv_rows.reshape(groups * capacity, hidden_part)

    member = jnp.arange(targets, dtype=jnp.int32)[:, None] == recv_slots[None, :]
    total = jnp.dot(member.astype(jnp.bfloat16), recv_rows, preferred_element_type=jnp.float32)
    count = jnp.sum(member.astype(jnp.float32), axis=1)
    neigh_h = (total / jnp.maximum(count, 1.0)[:, None]).astype(jnp.bfloat16)
    partial_two = jnp.dot(neigh_h, w2_neigh, preferred_element_type=jnp.float32)
    holds = (jnp.arange(parts) == me)[:, None, None]
    partial_two = partial_two.reshape(parts, own_part, hidden) + jnp.where(holds, own_two[None], 0.0)
    partial_two = partial_two.reshape(targets, parts, hidden_part).transpose(1, 0, 2)
    shared = lax.all_to_all(partial_two, "feat", split_axis=0, concat_axis=0, tiled=True)
    return (jnp.sum(shared, axis=0) + b2_bias).astype(jnp.bfloat16)


def solution(mesh):
    in_specs = (
        P(None, "feat"),
        P("grp", "feat"),
        P("grp", None, None),
        P("grp", None),
        P("grp"),
        P("grp", None),
        P("grp", None),
        P("grp"),
        P("feat", None),
        P("feat", None),
        P("feat"),
        P("feat", None),
        P("feat", None),
        P("feat"),
    )
    out_specs = P("grp", "feat")
    return jax.shard_map(
        per_device, mesh=mesh, in_specs=in_specs, out_specs=out_specs, check_vma=False
    )
```

```python
import functools

import jax
import jax.numpy as jnp
from jax import lax
from jax.experimental import pallas as pl
from jax.experimental.pallas import tpu as pltpu
from jax.sharding import PartitionSpec as P


BLK = 128
LANES = 128
HOT = 16384
MAIN = 480
PREFIX_AT = 32
FLAG_AT = 64


def mark_kernel(refs, before, owners, extras, notes, look, acc):
    owner_rows = before.shape[0]
    groups = notes.shape[0]
    slot_count = owner_rows // groups
    acc[...] = jnp.zeros_like(acc)
    high = lax.broadcasted_iota(jnp.int32, (owner_rows, LANES), 0)
    low = lax.broadcasted_iota(jnp.int32, (LANES, LANES), 0)

    def count(g, carry):
        tall, wide = [], []
        for j in range(2):
            cold = refs[pl.ds(2 * g + j, 1), :] - HOT
            tall.append(jnp.where(high == cold >> 7, 1.0, 0.0).astype(jnp.bfloat16))
            wide.append(jnp.where(low == (cold & 127), 1.0, 0.0).astype(jnp.bfloat16))
        acc[...] += lax.dot_general(
            jnp.concatenate(tall, axis=1),
            jnp.concatenate(wide, axis=1),
            (((1,), (1,)), ((), ())),
            preferred_element_type=jnp.float32,
        )
        return carry

    lax.fori_loop(0, refs.shape[0] // 2, count, 0, unroll=11)
    needed = jnp.where(acc[...] > 0.0, 1.0, 0.0)
    upto = jnp.where(low <= lax.broadcasted_iota(jnp.int32, (LANES, LANES), 1), 1.0, 0.0)
    running = jnp.dot(
        needed.astype(jnp.bfloat16), upto.astype(jnp.bfloat16), preferred_element_type=jnp.float32
    )
    totals = jnp.dot(
        needed.astype(jnp.bfloat16),
        jnp.ones((LANES, LANES), jnp.bfloat16),
        preferred_element_type=jnp.float32,
    )
    earlier = jnp.dot(before[...], totals.astype(jnp.bfloat16), preferred_element_type=jnp.float32)
    local = jnp.where(needed > 0.0, running - 1.0, -1.0)
    place = jnp.where(needed > 0.0, earlier + running - 1.0, -1.0)
    spills = jnp.where(jnp.max(place) >= MAIN, 1, 0)
    place = place.astype(jnp.int32)
    lane = lax.broadcasted_iota(jnp.int32, (slot_count, LANES), 1)
    slot_lane = lane - PREFIX_AT == lax.broadcasted_iota(jnp.int32, (slot_count, LANES), 0)
    row_lane = lax.broadcasted_iota(jnp.int32, (1, LANES), 1)
    for o in range(groups):
        span = slice(o * slot_count, (o + 1) * slot_count)
        notes[o, 0:slot_count, :] = place[span]
        prefix = jnp.sum(jnp.where(slot_lane, earlier[span], 0.0), axis=0, keepdims=True)
        last = jnp.where(row_lane < PREFIX_AT, extras[o, 1:2, :], prefix.astype(jnp.int32))
        notes[o, slot_count : slot_count + 1, :] = extras[o, 0:1, :]
        notes[o, slot_count + 1 : slot_count + 2, :] = jnp.where(row_lane >= FLAG_AT, spills, last)
    across = jnp.transpose(earlier)[0:1]
    eighth = jnp.floor(across * 0.125)
    rest = jnp.zeros((5, owner_rows), jnp.float32)
    rows = [jnp.transpose(local), owners[0:1, :], eighth, across - 8.0 * eighth, rest]
    look[...] = jnp.concatenate(rows, axis=0).astype(jnp.bfloat16)


def mark_rows(refs, extras, slot_count, groups):
    rows = groups * slot_count
    at = jnp.arange(rows, dtype=jnp.int32)
    before = (at[:, None] // slot_count == at[None, :] // slot_count) & (at[None, :] < at[:, None])
    owners = jnp.broadcast_to((at // slot_count).astype(jnp.float32)[None, :], (8, rows))
    return pl.pallas_call(
        mark_kernel,
        out_shape=(
            jax.ShapeDtypeStruct((groups, slot_count + 2, LANES), jnp.int32),
            jax.ShapeDtypeStruct((LANES + 8, rows), jnp.bfloat16),
        ),
        in_specs=[pl.BlockSpec(memory_space=pltpu.VMEM)] * 4,
        out_specs=(pl.BlockSpec(memory_space=pltpu.VMEM),) * 2,
        scratch_shapes=[pltpu.VMEM((rows, LANES), jnp.float32)],
        name="mark_rows",
    )(refs, before.astype(jnp.bfloat16), owners, extras)


def remap_kernel(spill, groups, refs, look, *outs):
    owner_rows = look.shape[1]
    high = lax.broadcasted_iota(jnp.int32, (owner_rows, LANES), 0)
    low = lax.broadcasted_iota(jnp.int32, (LANES, LANES), 0)
    rows = outs[0].shape[0]
    table = look[...]
    for k, out in enumerate(outs):

        def lookup(g, carry, k=k, out=out):
            names = [refs[pl.ds(k * rows + 2 * g + j, 1), :] for j in range(2)]
            tall = [
                jnp.where(high == (name - HOT) >> 7, 1.0, 0.0).astype(jnp.bfloat16)
                for name in names
            ]
            found = jnp.dot(
                table, jnp.concatenate(tall, axis=1), preferred_element_type=jnp.float32
            )
            for j, name in enumerate(names):
                part = found[:, j * LANES : (j + 1) * LANES]
                local = jnp.where(low == ((name - HOT) & 127), part[:LANES], 0.0)
                local = jnp.sum(local, axis=0, keepdims=True)
                owner, eighth, unit = (part[LANES + n : LANES + n + 1] for n in range(3))
                place = 8.0 * eighth + unit + local
                cold = jnp.where(
                    place < MAIN,
                    HOT + owner * MAIN + place,
                    HOT + groups * MAIN + owner * spill + place - MAIN,
                ).astype(jnp.int32)
                out[pl.ds(2 * g + j, 1), :] = jnp.where(name < HOT, name, cold) * 2
            return carry

        lax.fori_loop(0, rows // 2, lookup, 0, unroll=11)


def remap(refs, look, nodes, spill, groups):
    count = refs.shape[0] * LANES // nodes
    outs = pl.pallas_call(
        functools.partial(remap_kernel, spill, groups),
        out_shape=[jax.ShapeDtypeStruct((nodes // LANES, LANES), jnp.int32)] * count,
        in_specs=[pl.BlockSpec(memory_space=pltpu.VMEM)] * 2,
        out_specs=[pl.BlockSpec(memory_space=pltpu.VMEM)] * count,
        name="remap",
    )(refs, look)
    return tuple(out.reshape(nodes) for out in outs)


def pack_kernel(first, slot_count, blocks, counts, prefix, need, cold, out, left, right):
    r = pl.program_id(0)
    rows = out.shape[1]
    at = lax.broadcasted_iota(jnp.int32, (BLK, BLK), 0)
    for k in range(slot_count):
        begin = prefix[r * slot_count + k]
        place = need[0, k : k + 1, :] - begin
        place = jnp.where(counts[r] > k, place, -1)
        picks = jnp.where(at == place, 1.0, 0.0).astype(jnp.bfloat16)
        origin = pl.multiple_of(blocks[r * slot_count + k] * BLK, BLK)
        value = jnp.dot(picks, cold[pl.ds(origin, BLK), :], preferred_element_type=jnp.float32)
        left[pl.ds(begin, BLK), :] = value[:, :LANES]
        right[pl.ds(begin, BLK), :] = value[:, LANES:]
    out[0, :, :LANES] = left[first : first + rows, :].astype(out.dtype)
    out[0, :, LANES:] = right[first : first + rows, :].astype(out.dtype)


def pack_needed(blocks, counts, prefix, need, cold, first, rows):
    groups = counts.shape[0]
    cols = cold.shape[1]
    slot_count = blocks.shape[0] // groups
    return pl.pallas_call(
        functools.partial(pack_kernel, first, slot_count),
        grid=(groups,),
        out_shape=jax.ShapeDtypeStruct((groups, rows, cols), cold.dtype),
        in_specs=[
            pl.BlockSpec(memory_space=pltpu.SMEM),
            pl.BlockSpec(memory_space=pltpu.SMEM),
            pl.BlockSpec(memory_space=pltpu.SMEM),
            pl.BlockSpec((1,) + need.shape[1:], lambda r: (r, 0, 0)),
            pl.BlockSpec(memory_space=pltpu.VMEM),
        ],
        out_specs=pl.BlockSpec((1, rows, cols), lambda r: (r, 0, 0)),
        scratch_shapes=[pltpu.VMEM((slot_count * BLK + BLK, LANES), jnp.float32)] * 2,
        name="pack_needed",
    )(blocks, counts, prefix, need, cold)


def layer_one_kernel(parts, me, base, *refs):
    own, mean, weights = (refs[n * parts : (n + 1) * parts] for n in range(3))
    out, own_two, hidden, bias, product = refs[3 * parts :]
    half = own[0].shape[1]
    depth = 2 * half
    width = weights[0].shape[1]
    groups, _, slots, cols = out.shape
    own_part = own_two.shape[0]
    total_rows = own[0].shape[0]
    sources = [lax.rem(me[0] - step + parts, parts) for step in range(parts)]
    for source, weight in zip(sources, weights):
        tail = weight[depth + cols : depth + cols + 8, :cols].astype(jnp.float32)
        bias[:, pl.ds(pl.multiple_of(source * cols, cols), cols)] = (
            tail[0:1] + tail[1:2] + tail[2:3]
        )
    chunk = total_rows // 4
    for c in range(4):
        span = slice(c * chunk, (c + 1) * chunk)
        pre = jnp.broadcast_to(bias[...], (chunk, width))
        for self_x, neigh_x, weight in zip(own, mean, weights):
            pre = pre + jnp.dot(
                self_x[span, :], weight[0:half, :], preferred_element_type=jnp.float32
            )
            pre = pre + jnp.dot(
                neigh_x[span, :], weight[half:depth, :], preferred_element_type=jnp.float32
            )
        h1 = jnp.maximum(pre, 0.0).astype(jnp.bfloat16).astype(jnp.float32)
        for f in range(parts):
            hidden[f, span, :] = h1[:, f * cols : (f + 1) * cols]
    for f in range(parts):
        hidden[f, total_rows:, :] = jnp.zeros((hidden.shape[1] - total_rows, cols), jnp.float32)
    total = jnp.zeros((own_part, width), jnp.float32)
    for source, weight in zip(sources, weights):
        total = total + jnp.dot(
            hidden[source, 0:own_part, :].astype(jnp.bfloat16),
            weight[depth : depth + cols, :],
            preferred_element_type=jnp.float32,
        )
    product[...] = total
    for step in range(parts):
        column = pl.multiple_of(lax.rem(me[0] + step, parts) * cols, cols)
        own_two[:, step * cols : (step + 1) * cols] = product[:, pl.ds(column, cols)]

    def send(o, carry):
        for f in range(parts):
            out[o, f] = hidden[f, pl.ds(base[o], slots), :].astype(out.dtype)
        return carry

    lax.fori_loop(0, groups, send, 0)


def layer_one(me, base, own, mean, weights, groups, slots, own_part):
    parts = len(weights)
    total_rows = own[0].shape[0]
    width = weights[0].shape[1]
    cols = width // parts
    return pl.pallas_call(
        functools.partial(layer_one_kernel, parts),
        out_shape=(
            jax.ShapeDtypeStruct((groups, parts, slots, cols), jnp.bfloat16),
            jax.ShapeDtypeStruct((own_part, width), jnp.float32),
        ),
        in_specs=[pl.BlockSpec(memory_space=pltpu.SMEM)] * 2
        + [pl.BlockSpec(memory_space=pltpu.VMEM)] * (3 * parts),
        out_specs=(pl.BlockSpec(memory_space=pltpu.VMEM),) * 2,
        scratch_shapes=[
            pltpu.VMEM((parts, total_rows + slots, cols), jnp.float32),
            pltpu.VMEM((1, width), jnp.float32),
            pltpu.VMEM((own_part, width), jnp.float32),
        ],
        name="layer_one",
    )(me, base, *own, *mean, *weights)


CHUNK = 1024
DEPTH = 4


def gather_kernel(columns, source_count, dest, extent, *refs):
    index, refs = refs[:columns], refs[columns:]
    sources, refs = refs[:source_count], refs[source_count:]
    outs, (table, stage, acc, sems) = refs[:-4], refs[-4:]
    chunks = extent[0]
    nodes = dest.shape[0]

    def copy(c, slot):
        begin = 0
        for source in sources:
            length = source.shape[0] // CHUNK
            first = begin

            @pl.when((c >= first) & (c < first + length))
            def _():
                rows = pl.ds(pl.multiple_of((c - first) * CHUNK, CHUNK), CHUNK)
                pltpu.make_async_copy(source.at[rows], stage.at[slot], sems.at[slot]).start()

            begin += length

    for c in range(DEPTH):
        copy(c, c)

    def fill(i, carry):
        acc[pl.ds(pl.multiple_of(i * 8, 8), 8), :] = jnp.zeros((8, LANES), jnp.float32)
        return carry

    lax.fori_loop(0, acc.shape[0] // 8, fill, 0, unroll=8)

    def load(c, carry):
        slot = lax.rem(c, DEPTH)
        pltpu.make_async_copy(sources[0].at[pl.ds(0, CHUNK)], stage.at[slot], sems.at[slot]).wait()

        def widen(g, inner):
            value = stage[slot, pl.ds(pl.multiple_of(g * 16, 16), 16), :].astype(jnp.float32)
            row = pl.multiple_of(c * (2 * CHUNK) + g * 32, 32)
            table[pl.ds(row, 16, stride=2), :] = value[:, :LANES]
            table[pl.ds(row + 1, 16, stride=2), :] = value[:, LANES:]
            return inner

        lax.fori_loop(0, CHUNK // 16, widen, 0, unroll=4)

        @pl.when(c + DEPTH < chunks)
        def _():
            copy(c + DEPTH, slot)

        return carry

    lax.fori_loop(0, chunks, load, 0)

    def node(i, carry):
        rows = [table[pl.ds(pl.multiple_of(column[i], 2), 2), :] for column in index]
        while len(rows) > 1:
            rows = [a + b for a, b in zip(rows[::2], rows[1::2])] + rows[len(rows) // 2 * 2 :]
        acc[pl.ds(pl.multiple_of(dest[i], 2), 2), :] = rows[0]
        return carry

    lax.fori_loop(0, nodes, node, 0, unroll=8)

    for f, out in enumerate(outs):
        first = 2 * f * out.shape[0]

        def finish(g, carry, first=first, out=out):
            row = pl.multiple_of(first + g * 32, 32)
            halves = [acc[pl.ds(row + j, 16, stride=2), :] for j in range(2)]
            if columns > 1:
                halves = [half / columns for half in halves]
            out[pl.ds(pl.multiple_of(g * 16, 16), 16), :] = jnp.concatenate(halves, axis=1).astype(
                jnp.bfloat16
            )
            return carry

        lax.fori_loop(0, out.shape[0] // 16, finish, 0, unroll=2)


def gather_rows(index, dest, extent, sources, parts, rows):
    cols = sources[0].shape[1]
    table_rows = sum(source.shape[0] for source in sources)
    return pl.pallas_call(
        functools.partial(gather_kernel, len(index), len(sources)),
        out_shape=[jax.ShapeDtypeStruct((rows, cols), jnp.bfloat16)] * parts,
        in_specs=[pl.BlockSpec(memory_space=pltpu.SMEM)] * (2 + len(index))
        + [pl.BlockSpec(memory_space=pl.ANY)] * len(sources),
        out_specs=[pl.BlockSpec(memory_space=pltpu.VMEM)] * parts,
        scratch_shapes=[
            pltpu.VMEM((2 * table_rows, LANES), jnp.float32),
            pltpu.VMEM((DEPTH, CHUNK, cols), jnp.bfloat16),
            pltpu.VMEM((2 * parts * rows, LANES), jnp.float32),
            pltpu.SemaphoreType.DMA((DEPTH,)),
        ],
        compiler_params=pltpu.CompilerParams(vmem_limit_bytes=60 * 1024 * 1024),
    )(dest, extent, *index, *sources)


def unused_kernel(out):
    out[...] = jnp.zeros_like(out)


def unused_rows(rows, cols, dtype):
    return pl.pallas_call(
        unused_kernel,
        grid=(1,),
        out_shape=jax.ShapeDtypeStruct((rows, cols), dtype),
        out_specs=pl.BlockSpec((16, cols), lambda i: (0, 0)),
        name="unused_rows",
    )()


def send_round(chunks):
    parts = len(chunks)
    received = [chunks[0]]
    for step in range(1, parts):
        ring = [(s, (s + step) % parts) for s in range(parts)]
        received.append(lax.ppermute(chunks[step], "feat", ring))
    return received


def per_device(
    hot_table,
    cold_table,
    send_blocks,
    block_counts,
    self_ref,
    neigh_ref,
    route_owner,
    route_slot,
    w1_self,
    w1_neigh,
    b1_bias,
    w2_self,
    w2_neigh,
    b2_bias,
):
    groups = lax.axis_size("grp")
    parts = lax.axis_size("feat")
    me = lax.axis_index("feat")
    routed = route_slot.shape[0]
    nodes = self_ref.shape[0]
    targets = nodes - routed
    own_part = targets // parts
    hidden = w1_self.shape[1]
    hidden_part = b1_bias.shape[0]
    capacity = 2 * routed // groups
    slots = capacity // parts
    part_rows = own_part + (routed + (parts - 1) * groups) // parts
    part_rows = (part_rows + 15) // 16 * 16

    feat_cols = cold_table.shape[1]
    slot_count = send_blocks.shape[2]
    fetch_rows = slot_count * BLK
    refs = jnp.concatenate([self_ref, neigh_ref.T.reshape(-1)]).reshape(-1, LANES)

    coarse = lax.reduce_precision(b1_bias, 8, 7)
    middle = lax.reduce_precision(b1_bias - coarse, 8, 7)
    fine = b1_bias - coarse - middle
    bias_rows = jnp.stack([coarse, middle, fine]).astype(jnp.bfloat16)
    bias_rows = jnp.pad(bias_rows, ((0, 16 - 3), (0, hidden - hidden_part)))
    weight = jnp.concatenate([w1_self, w1_neigh, w2_self, bias_rows], axis=0)
    weights = [weight]
    for step in range(1, parts):
        ring = [(s, (s + step) % parts) for s in range(parts)]
        weights.append(lax.ppermute(weight, "feat", ring))

    owner = route_owner[:, 0]
    onehot = (owner[:, None] == jnp.arange(groups, dtype=jnp.int32)[None, :]).astype(jnp.int32)
    spans = routed // LANES
    upto = jnp.arange(LANES)[:, None] <= jnp.arange(LANES)[None, :]
    running = jnp.dot(
        onehot.T.astype(jnp.bfloat16).reshape(groups * spans, LANES),
        upto.astype(jnp.bfloat16),
        preferred_element_type=jnp.float32,
    ).reshape(groups, spans, LANES)
    span_totals = running[:, :, -1]
    before = jnp.arange(spans)[:, None] < jnp.arange(spans)[None, :]
    earlier = jnp.dot(
        span_totals.astype(jnp.bfloat16), before.astype(jnp.bfloat16), preferred_element_type=jnp.float32
    )
    ranks = (running + earlier[:, :, None]).astype(jnp.int32).reshape(groups, routed)
    position = jnp.sum((ranks - 1) * onehot.T, axis=0)
    quarter, depth = position % parts, position // parts
    totals = ranks[:, -1]
    held = (totals[None, :] - jnp.arange(parts)[:, None] + parts - 1) // parts
    base = jnp.cumsum(held, axis=1) - held + own_part
    owner_base = jnp.sum(onehot[:, :, None] * base.T[None, :, :], axis=1)
    mine = quarter[:, None] == jnp.arange(parts)[None, :]
    row_base = jnp.sum(jnp.where(mine, owner_base, 0), axis=1)
    routed_dest = (quarter - me + parts) % parts * part_rows + row_base + depth
    own = jnp.arange(targets, dtype=jnp.int32)
    own_dest = (own // own_part - me + parts) % parts * part_rows + own % own_part
    dest = jnp.concatenate([own_dest, routed_dest]) * 2

    column = quarter * slots + depth
    named = (column[:, None] == jnp.arange(capacity, dtype=jnp.int32)[None, :]).astype(jnp.bfloat16)
    send_slots = lax.dot_general(
        onehot.astype(jnp.bfloat16),
        named * (route_slot + 1).astype(jnp.bfloat16)[:, None],
        (((0,), (0,)), ((), ())),
        preferred_element_type=jnp.float32,
    )
    send_slots = send_slots.astype(jnp.int32) - 1
    extras = jnp.pad(send_slots, ((0, 0), (0, 2 * LANES - capacity))).reshape(groups, 2, LANES)
    notes, look = mark_rows(refs, extras, slot_count, groups)
    notes = lax.all_to_all(notes, "grp", split_axis=0, concat_axis=0, tiled=True)
    spill = fetch_rows - MAIN
    index = remap(refs, look, nodes, spill, groups)
    recv_slots = notes[:, slot_count:, :].reshape(groups, -1)[:, :capacity]
    recv_slots = recv_slots.reshape(groups * capacity)
    spilled = jnp.max(notes[:, slot_count + 1, FLAG_AT]) > 0
    prefix = notes[:, slot_count + 1, PREFIX_AT : PREFIX_AT + slot_count].reshape(-1)

    def exchange(first, rows, prepared):
        outgoing = pack_needed(
            send_blocks.reshape(-1),
            block_counts.reshape(-1),
            prefix,
            notes,
            cold_table,
            first,
            rows,
        )
        outgoing, prepared = lax.optimization_barrier((outgoing, prepared))
        fetched = lax.all_to_all(outgoing, "grp", split_axis=0, concat_axis=0, tiled=True)
        fetched, prepared = lax.optimization_barrier((fetched, prepared))
        return fetched.reshape(-1, feat_cols), prepared

    my_base = lax.dynamic_index_in_dim(base, me, 0, keepdims=False)

    turned = lax.dynamic_slice_in_dim(
        jnp.concatenate([w2_neigh, w2_neigh], axis=1), me * hidden_part, hidden, 1
    )
    prepared = (weights, index, dest, recv_slots, my_base, spilled, turned)
    main, prepared = exchange(0, MAIN, prepared)
    weights, index, dest, recv_slots, my_base, spilled, turned = prepared

    extent = (HOT + groups * MAIN + jnp.where(spilled, groups * spill, 0)) // CHUNK
    extent = extent.astype(jnp.int32).reshape(1)

    def gather_own(extra):
        own = gather_rows(index[:1], dest, extent, [hot_table, main, extra], parts, part_rows)
        return own, extra

    own_rows, extra = lax.cond(
        spilled,
        lambda: gather_own(exchange(MAIN, spill, ())[0]),
        lambda: gather_own(unused_rows(groups * spill, feat_cols, cold_table.dtype)),
    )
    sources = [hot_table, main, extra]
    own_rows, others = lax.optimization_barrier((own_rows, index[1:]))
    own_rows = send_round(own_rows)
    mean_rows = gather_rows(others, dest, extent, sources, parts, part_rows)
    mean_rows = send_round(mean_rows)
    send_rows, own_two = layer_one(
        me.reshape(1), my_base, own_rows, mean_rows, weights, groups, slots, own_part
    )
    send_rows = send_rows.reshape(groups * parts, slots, hidden_part)
    recv_rows = lax.all_to_all(send_rows, ("grp", "feat"), split_axis=0, concat_axis=0, tiled=True)
    recv_rows = recv_rows.reshape(groups * capacity, hidden_part)

    member = jnp.arange(targets, dtype=jnp.int32)[:, None] == recv_slots[None, :]
    total = jnp.dot(member.astype(jnp.bfloat16), recv_rows, preferred_element_type=jnp.float32)
    count = jnp.sum(member.astype(jnp.float32), axis=1)
    neigh_h = (total / jnp.maximum(count, 1.0)[:, None]).astype(jnp.bfloat16)
    partial_two = jnp.dot(neigh_h, turned, preferred_element_type=jnp.float32)
    holds = (jnp.arange(parts) == me)[:, None, None]
    partial_two = partial_two.reshape(parts, own_part, hidden) + jnp.where(holds, own_two[None], 0.0)
    partial_two = partial_two.reshape(targets, hidden)
    shared = send_round(jnp.split(partial_two, parts, axis=1))
    return (sum(shared[1:], shared[0]) + b2_bias).astype(jnp.bfloat16)


def solution(mesh):
    in_specs = (
        P(None, "feat"),
        P("grp", "feat"),
        P("grp", None, None),
        P("grp", None),
        P("grp"),
        P("grp", None),
        P("grp", None),
        P("grp"),
        P("feat", None),
        P("feat", None),
        P("feat"),
        P("feat", None),
        P("feat", None),
        P("feat"),
    )
    out_specs = P("grp", "feat")
    return jax.shard_map(
        per_device, mesh=mesh, in_specs=in_specs, out_specs=out_specs, check_vma=False
    )
```

```python
import functools

import jax
import jax.numpy as jnp
from jax import lax
from jax.experimental import pallas as pl
from jax.experimental.pallas import tpu as pltpu
from jax.sharding import PartitionSpec as P


BLK = 128
LANES = 128
HOT = 16384
MAIN = 480
PREFIX_AT = 32
FLAG_AT = 64


def mark_kernel(refs, before, owners, extras, notes, look, acc):
    owner_rows = before.shape[0]
    groups = notes.shape[0]
    slot_count = owner_rows // groups
    acc[...] = jnp.zeros_like(acc)
    high = lax.broadcasted_iota(jnp.int32, (owner_rows, LANES), 0)
    low = lax.broadcasted_iota(jnp.int32, (LANES, LANES), 0)

    def count(g, carry):
        tall, wide = [], []
        for j in range(2):
            cold = refs[pl.ds(2 * g + j, 1), :] - HOT
            tall.append(jnp.where(high == cold >> 7, 1.0, 0.0).astype(jnp.bfloat16))
            wide.append(jnp.where(low == (cold & 127), 1.0, 0.0).astype(jnp.bfloat16))
        acc[...] += lax.dot_general(
            jnp.concatenate(tall, axis=1),
            jnp.concatenate(wide, axis=1),
            (((1,), (1,)), ((), ())),
            preferred_element_type=jnp.float32,
        )
        return carry

    lax.fori_loop(0, refs.shape[0] // 2, count, 0, unroll=11)
    needed = jnp.where(acc[...] > 0.0, 1.0, 0.0)
    upto = jnp.where(low <= lax.broadcasted_iota(jnp.int32, (LANES, LANES), 1), 1.0, 0.0)
    running = jnp.dot(
        needed.astype(jnp.bfloat16), upto.astype(jnp.bfloat16), preferred_element_type=jnp.float32
    )
    totals = jnp.dot(
        needed.astype(jnp.bfloat16),
        jnp.ones((LANES, LANES), jnp.bfloat16),
        preferred_element_type=jnp.float32,
    )
    earlier = jnp.dot(before[...], totals.astype(jnp.bfloat16), preferred_element_type=jnp.float32)
    local = jnp.where(needed > 0.0, running - 1.0, -1.0)
    place = jnp.where(needed > 0.0, earlier + running - 1.0, -1.0)
    spills = jnp.where(jnp.max(place) >= MAIN, 1, 0)
    place = place.astype(jnp.int32)
    lane = lax.broadcasted_iota(jnp.int32, (slot_count, LANES), 1)
    slot_lane = lane - PREFIX_AT == lax.broadcasted_iota(jnp.int32, (slot_count, LANES), 0)
    row_lane = lax.broadcasted_iota(jnp.int32, (1, LANES), 1)
    for o in range(groups):
        span = slice(o * slot_count, (o + 1) * slot_count)
        notes[o, 0:slot_count, :] = place[span]
        prefix = jnp.sum(jnp.where(slot_lane, earlier[span], 0.0), axis=0, keepdims=True)
        last = jnp.where(row_lane < PREFIX_AT, extras[o, 1:2, :], prefix.astype(jnp.int32))
        notes[o, slot_count : slot_count + 1, :] = extras[o, 0:1, :]
        notes[o, slot_count + 1 : slot_count + 2, :] = jnp.where(row_lane >= FLAG_AT, spills, last)
    across = jnp.transpose(earlier)[0:1]
    eighth = jnp.floor(across * 0.125)
    rest = jnp.zeros((5, owner_rows), jnp.float32)
    rows = [jnp.transpose(local), owners[0:1, :], eighth, across - 8.0 * eighth, rest]
    look[...] = jnp.concatenate(rows, axis=0).astype(jnp.bfloat16)


def mark_rows(refs, extras, slot_count, groups):
    rows = groups * slot_count
    at = jnp.arange(rows, dtype=jnp.int32)
    before = (at[:, None] // slot_count == at[None, :] // slot_count) & (at[None, :] < at[:, None])
    owners = jnp.broadcast_to((at // slot_count).astype(jnp.float32)[None, :], (8, rows))
    return pl.pallas_call(
        mark_kernel,
        out_shape=(
            jax.ShapeDtypeStruct((groups, slot_count + 2, LANES), jnp.int32),
            jax.ShapeDtypeStruct((LANES + 8, rows), jnp.bfloat16),
        ),
        in_specs=[pl.BlockSpec(memory_space=pltpu.VMEM)] * 4,
        out_specs=(pl.BlockSpec(memory_space=pltpu.VMEM),) * 2,
        scratch_shapes=[pltpu.VMEM((rows, LANES), jnp.float32)],
        name="mark_rows",
    )(refs, before.astype(jnp.bfloat16), owners, extras)


def remap_kernel(spill, groups, refs, look, *outs):
    owner_rows = look.shape[1]
    high = lax.broadcasted_iota(jnp.int32, (owner_rows, LANES), 0)
    low = lax.broadcasted_iota(jnp.int32, (LANES, LANES), 0)
    rows = outs[0].shape[0]
    table = look[...]
    for k, out in enumerate(outs):

        def lookup(g, carry, k=k, out=out):
            names = [refs[pl.ds(k * rows + 2 * g + j, 1), :] for j in range(2)]
            tall = [
                jnp.where(high == (name - HOT) >> 7, 1.0, 0.0).astype(jnp.bfloat16)
                for name in names
            ]
            found = jnp.dot(
                table, jnp.concatenate(tall, axis=1), preferred_element_type=jnp.float32
            )
            for j, name in enumerate(names):
                part = found[:, j * LANES : (j + 1) * LANES]
                local = jnp.where(low == ((name - HOT) & 127), part[:LANES], 0.0)
                local = jnp.sum(local, axis=0, keepdims=True)
                owner, eighth, unit = (part[LANES + n : LANES + n + 1] for n in range(3))
                place = 8.0 * eighth + unit + local
                cold = jnp.where(
                    place < MAIN,
                    HOT + owner * MAIN + place,
                    HOT + groups * MAIN + owner * spill + place - MAIN,
                ).astype(jnp.int32)
                out[pl.ds(2 * g + j, 1), :] = jnp.where(name < HOT, name, cold) * 2
            return carry

        lax.fori_loop(0, rows // 2, lookup, 0, unroll=11)


def remap(refs, look, nodes, spill, groups):
    count = refs.shape[0] * LANES // nodes
    outs = pl.pallas_call(
        functools.partial(remap_kernel, spill, groups),
        out_shape=[jax.ShapeDtypeStruct((nodes // LANES, LANES), jnp.int32)] * count,
        in_specs=[pl.BlockSpec(memory_space=pltpu.VMEM)] * 2,
        out_specs=[pl.BlockSpec(memory_space=pltpu.VMEM)] * count,
        name="remap",
    )(refs, look)
    return tuple(out.reshape(nodes) for out in outs)


TOGETHER = 4


def pack_kernel(first, slot_count, blocks, counts, prefix, need, cold, out, left, right):
    rows = out.shape[1]
    at = lax.broadcasted_iota(jnp.int32, (BLK, BLK), 0)
    for n in range(TOGETHER):
        r = pl.program_id(0) * TOGETHER + n
        for k in range(slot_count):
            begin = prefix[r * slot_count + k]
            place = need[n, k : k + 1, :] - begin
            place = jnp.where(counts[r] > k, place, -1)
            picks = jnp.where(at == place, 1.0, 0.0).astype(jnp.bfloat16)
            origin = pl.multiple_of(blocks[r * slot_count + k] * BLK, BLK)
            value = jnp.dot(picks, cold[pl.ds(origin, BLK), :], preferred_element_type=jnp.float32)
            left[n, pl.ds(begin, BLK), :] = value[:, :LANES]
            right[n, pl.ds(begin, BLK), :] = value[:, LANES:]
    for n in range(TOGETHER):
        out[n, :, :LANES] = left[n, first : first + rows, :].astype(out.dtype)
        out[n, :, LANES:] = right[n, first : first + rows, :].astype(out.dtype)


def pack_needed(blocks, counts, prefix, need, cold, first, rows):
    groups = counts.shape[0]
    cols = cold.shape[1]
    slot_count = blocks.shape[0] // groups
    return pl.pallas_call(
        functools.partial(pack_kernel, first, slot_count),
        grid=(groups // TOGETHER,),
        out_shape=jax.ShapeDtypeStruct((groups, rows, cols), cold.dtype),
        in_specs=[
            pl.BlockSpec(memory_space=pltpu.SMEM),
            pl.BlockSpec(memory_space=pltpu.SMEM),
            pl.BlockSpec(memory_space=pltpu.SMEM),
            pl.BlockSpec((TOGETHER,) + need.shape[1:], lambda r: (r, 0, 0)),
            pl.BlockSpec(memory_space=pltpu.VMEM),
        ],
        out_specs=pl.BlockSpec((TOGETHER, rows, cols), lambda r: (r, 0, 0)),
        scratch_shapes=[pltpu.VMEM((TOGETHER, slot_count * BLK + BLK, LANES), jnp.float32)] * 2,
        name="pack_needed",
    )(blocks, counts, prefix, need, cold)


def layer_one_kernel(parts, me, base, *refs):
    own, mean, weights = (refs[n * parts : (n + 1) * parts] for n in range(3))
    out, own_two, hidden, bias, product = refs[3 * parts :]
    half = own[0].shape[1]
    depth = 2 * half
    width = weights[0].shape[1]
    groups, _, slots, cols = out.shape
    own_part = own_two.shape[0]
    total_rows = own[0].shape[0]
    sources = [lax.rem(me[0] - step + parts, parts) for step in range(parts)]
    for source, weight in zip(sources, weights):
        tail = weight[depth + cols : depth + cols + 8, :cols].astype(jnp.float32)
        bias[:, pl.ds(pl.multiple_of(source * cols, cols), cols)] = (
            tail[0:1] + tail[1:2] + tail[2:3]
        )
    chunk = total_rows // 4
    for c in range(4):
        span = slice(c * chunk, (c + 1) * chunk)
        pre = jnp.broadcast_to(bias[...], (chunk, width))
        for self_x, neigh_x, weight in zip(own, mean, weights):
            pre = pre + jnp.dot(
                self_x[span, :], weight[0:half, :], preferred_element_type=jnp.float32
            )
            pre = pre + jnp.dot(
                neigh_x[span, :], weight[half:depth, :], preferred_element_type=jnp.float32
            )
        h1 = jnp.maximum(pre, 0.0).astype(jnp.bfloat16).astype(jnp.float32)
        for f in range(parts):
            hidden[f, span, :] = h1[:, f * cols : (f + 1) * cols]
    for f in range(parts):
        hidden[f, total_rows:, :] = jnp.zeros((hidden.shape[1] - total_rows, cols), jnp.float32)
    total = jnp.zeros((own_part, width), jnp.float32)
    for source, weight in zip(sources, weights):
        total = total + jnp.dot(
            hidden[source, 0:own_part, :].astype(jnp.bfloat16),
            weight[depth : depth + cols, :],
            preferred_element_type=jnp.float32,
        )
    product[...] = total
    for step in range(parts):
        column = pl.multiple_of(lax.rem(me[0] + step, parts) * cols, cols)
        own_two[:, step * cols : (step + 1) * cols] = product[:, pl.ds(column, cols)]

    def send(o, carry):
        for f in range(parts):
            out[o, f] = hidden[f, pl.ds(base[o], slots), :].astype(out.dtype)
        return carry

    lax.fori_loop(0, groups, send, 0)


def layer_one(me, base, own, mean, weights, groups, slots, own_part):
    parts = len(weights)
    total_rows = own[0].shape[0]
    width = weights[0].shape[1]
    cols = width // parts
    return pl.pallas_call(
        functools.partial(layer_one_kernel, parts),
        out_shape=(
            jax.ShapeDtypeStruct((groups, parts, slots, cols), jnp.bfloat16),
            jax.ShapeDtypeStruct((own_part, width), jnp.float32),
        ),
        in_specs=[pl.BlockSpec(memory_space=pltpu.SMEM)] * 2
        + [pl.BlockSpec(memory_space=pltpu.VMEM)] * (3 * parts),
        out_specs=(pl.BlockSpec(memory_space=pltpu.VMEM),) * 2,
        scratch_shapes=[
            pltpu.VMEM((parts, total_rows + slots, cols), jnp.float32),
            pltpu.VMEM((1, width), jnp.float32),
            pltpu.VMEM((own_part, width), jnp.float32),
        ],
        name="layer_one",
    )(me, base, *own, *mean, *weights)


CHUNK = 1024
DEPTH = 12


def gather_kernel(columns, source_count, dest, extent, *refs):
    index, refs = refs[:columns], refs[columns:]
    sources, refs = refs[:source_count], refs[source_count:]
    outs, (table, stage, acc, sems) = refs[:-4], refs[-4:]
    chunks = extent[0]
    nodes = dest.shape[0]

    def copy(c, slot):
        begin = 0
        for source in sources:
            length = source.shape[0] // CHUNK
            first = begin

            @pl.when((c >= first) & (c < first + length))
            def _():
                rows = pl.ds(pl.multiple_of((c - first) * CHUNK, CHUNK), CHUNK)
                pltpu.make_async_copy(source.at[rows], stage.at[slot], sems.at[slot]).start()

            begin += length

    for c in range(DEPTH):
        copy(c, c)

    def fill(i, carry):
        acc[pl.ds(pl.multiple_of(i * 8, 8), 8), :] = jnp.zeros((8, LANES), jnp.float32)
        return carry

    lax.fori_loop(0, acc.shape[0] // 8, fill, 0, unroll=8)

    def load(c, carry):
        slot = lax.rem(c, DEPTH)
        pltpu.make_async_copy(sources[0].at[pl.ds(0, CHUNK)], stage.at[slot], sems.at[slot]).wait()

        def widen(g, inner):
            value = stage[slot, pl.ds(pl.multiple_of(g * 16, 16), 16), :].astype(jnp.float32)
            row = pl.multiple_of(c * (2 * CHUNK) + g * 32, 32)
            table[pl.ds(row, 16, stride=2), :] = value[:, :LANES]
            table[pl.ds(row + 1, 16, stride=2), :] = value[:, LANES:]
            return inner

        lax.fori_loop(0, CHUNK // 16, widen, 0, unroll=8)

        @pl.when(c + DEPTH < chunks)
        def _():
            copy(c + DEPTH, slot)

        return carry

    lax.fori_loop(0, chunks, load, 0)

    def node(i, carry):
        rows = [table[pl.ds(pl.multiple_of(column[i], 2), 2), :] for column in index]
        while len(rows) > 1:
            rows = [a + b for a, b in zip(rows[::2], rows[1::2])] + rows[len(rows) // 2 * 2 :]
        acc[pl.ds(pl.multiple_of(dest[i], 2), 2), :] = rows[0]
        return carry

    lax.fori_loop(0, nodes, node, 0, unroll=8)

    for f, out in enumerate(outs):
        first = 2 * f * out.shape[0]

        def finish(g, carry, first=first, out=out):
            row = pl.multiple_of(first + g * 32, 32)
            halves = [acc[pl.ds(row + j, 16, stride=2), :] for j in range(2)]
            if columns > 1:
                halves = [half / columns for half in halves]
            out[pl.ds(pl.multiple_of(g * 16, 16), 16), :] = jnp.concatenate(halves, axis=1).astype(
                jnp.bfloat16
            )
            return carry

        lax.fori_loop(0, out.shape[0] // 16, finish, 0, unroll=2)


def gather_rows(index, dest, extent, sources, parts, rows):
    cols = sources[0].shape[1]
    table_rows = sum(source.shape[0] for source in sources)
    return pl.pallas_call(
        functools.partial(gather_kernel, len(index), len(sources)),
        out_shape=[jax.ShapeDtypeStruct((rows, cols), jnp.bfloat16)] * parts,
        in_specs=[pl.BlockSpec(memory_space=pltpu.SMEM)] * (2 + len(index))
        + [pl.BlockSpec(memory_space=pl.ANY)] * len(sources),
        out_specs=[pl.BlockSpec(memory_space=pltpu.VMEM)] * parts,
        scratch_shapes=[
            pltpu.VMEM((2 * table_rows, LANES), jnp.float32),
            pltpu.VMEM((DEPTH, CHUNK, cols), jnp.bfloat16),
            pltpu.VMEM((2 * parts * rows, LANES), jnp.float32),
            pltpu.SemaphoreType.DMA((DEPTH,)),
        ],
        compiler_params=pltpu.CompilerParams(vmem_limit_bytes=60 * 1024 * 1024),
    )(dest, extent, *index, *sources)


def unused_kernel(out):
    out[...] = jnp.zeros_like(out)


def unused_rows(rows, cols, dtype):
    return pl.pallas_call(
        unused_kernel,
        grid=(1,),
        out_shape=jax.ShapeDtypeStruct((rows, cols), dtype),
        out_specs=pl.BlockSpec((16, cols), lambda i: (0, 0)),
        name="unused_rows",
    )()


def send_round(chunks):
    parts = len(chunks)
    received = [chunks[0]]
    for step in range(1, parts):
        ring = [(s, (s + step) % parts) for s in range(parts)]
        received.append(lax.ppermute(chunks[step], "feat", ring))
    return received


def per_device(
    hot_table,
    cold_table,
    send_blocks,
    block_counts,
    self_ref,
    neigh_ref,
    route_owner,
    route_slot,
    w1_self,
    w1_neigh,
    b1_bias,
    w2_self,
    w2_neigh,
    b2_bias,
):
    groups = lax.axis_size("grp")
    parts = lax.axis_size("feat")
    me = lax.axis_index("feat")
    routed = route_slot.shape[0]
    nodes = self_ref.shape[0]
    targets = nodes - routed
    own_part = targets // parts
    hidden = w1_self.shape[1]
    hidden_part = b1_bias.shape[0]
    capacity = 2 * routed // groups
    slots = capacity // parts
    part_rows = own_part + (routed + (parts - 1) * groups) // parts
    part_rows = (part_rows + 15) // 16 * 16

    feat_cols = cold_table.shape[1]
    slot_count = send_blocks.shape[2]
    fetch_rows = slot_count * BLK
    refs = jnp.concatenate([self_ref, neigh_ref.T.reshape(-1)]).reshape(-1, LANES)

    coarse = lax.reduce_precision(b1_bias, 8, 7)
    middle = lax.reduce_precision(b1_bias - coarse, 8, 7)
    fine = b1_bias - coarse - middle
    bias_rows = jnp.stack([coarse, middle, fine]).astype(jnp.bfloat16)
    bias_rows = jnp.pad(bias_rows, ((0, 16 - 3), (0, hidden - hidden_part)))
    weight = jnp.concatenate([w1_self, w1_neigh, w2_self, bias_rows], axis=0)
    weights = [weight]
    for step in range(1, parts):
        ring = [(s, (s + step) % parts) for s in range(parts)]
        weights.append(lax.ppermute(weight, "feat", ring))

    owner = route_owner[:, 0]
    onehot = (owner[:, None] == jnp.arange(groups, dtype=jnp.int32)[None, :]).astype(jnp.int32)
    spans = routed // LANES
    upto = jnp.arange(LANES)[:, None] <= jnp.arange(LANES)[None, :]
    running = jnp.dot(
        onehot.T.astype(jnp.bfloat16).reshape(groups * spans, LANES),
        upto.astype(jnp.bfloat16),
        preferred_element_type=jnp.float32,
    ).reshape(groups, spans, LANES)
    span_totals = running[:, :, -1]
    before = jnp.arange(spans)[:, None] < jnp.arange(spans)[None, :]
    earlier = jnp.dot(
        span_totals.astype(jnp.bfloat16), before.astype(jnp.bfloat16), preferred_element_type=jnp.float32
    )
    ranks = (running + earlier[:, :, None]).astype(jnp.int32).reshape(groups, routed)
    position = jnp.sum((ranks - 1) * onehot.T, axis=0)
    quarter, depth = position % parts, position // parts
    totals = ranks[:, -1]
    held = (totals[None, :] - jnp.arange(parts)[:, None] + parts - 1) // parts
    base = jnp.cumsum(held, axis=1) - held + own_part
    owner_base = jnp.sum(onehot[:, :, None] * base.T[None, :, :], axis=1)
    mine = quarter[:, None] == jnp.arange(parts)[None, :]
    row_base = jnp.sum(jnp.where(mine, owner_base, 0), axis=1)
    routed_dest = (quarter - me + parts) % parts * part_rows + row_base + depth
    own = jnp.arange(targets, dtype=jnp.int32)
    own_dest = (own // own_part - me + parts) % parts * part_rows + own % own_part
    dest = jnp.concatenate([own_dest, routed_dest]) * 2

    column = quarter * slots + depth
    named = (column[:, None] == jnp.arange(capacity, dtype=jnp.int32)[None, :]).astype(jnp.bfloat16)
    send_slots = lax.dot_general(
        onehot.astype(jnp.bfloat16),
        named * (route_slot + 1).astype(jnp.bfloat16)[:, None],
        (((0,), (0,)), ((), ())),
        preferred_element_type=jnp.float32,
    )
    send_slots = send_slots.astype(jnp.int32) - 1
    extras = jnp.pad(send_slots, ((0, 0), (0, 2 * LANES - capacity))).reshape(groups, 2, LANES)
    notes, look = mark_rows(refs, extras, slot_count, groups)
    notes = lax.all_to_all(notes, "grp", split_axis=0, concat_axis=0, tiled=True)
    spill = fetch_rows - MAIN
    index = remap(refs, look, nodes, spill, groups)
    recv_slots = notes[:, slot_count:, :].reshape(groups, -1)[:, :capacity]
    recv_slots = recv_slots.reshape(groups * capacity)
    spilled = jnp.max(notes[:, slot_count + 1, FLAG_AT]) > 0
    prefix = notes[:, slot_count + 1, PREFIX_AT : PREFIX_AT + slot_count].reshape(-1)

    def exchange(first, rows, prepared):
        outgoing = pack_needed(
            send_blocks.reshape(-1),
            block_counts.reshape(-1),
            prefix,
            notes,
            cold_table,
            first,
            rows,
        )
        outgoing, prepared = lax.optimization_barrier((outgoing, prepared))
        fetched = lax.all_to_all(outgoing, "grp", split_axis=0, concat_axis=0, tiled=True)
        fetched, prepared = lax.optimization_barrier((fetched, prepared))
        return fetched.reshape(-1, feat_cols), prepared

    my_base = lax.dynamic_index_in_dim(base, me, 0, keepdims=False)

    turned = lax.dynamic_slice_in_dim(
        jnp.concatenate([w2_neigh, w2_neigh], axis=1), me * hidden_part, hidden, 1
    )
    prepared = (weights, index, dest, recv_slots, my_base, spilled, turned)
    main, prepared = exchange(0, MAIN, prepared)
    weights, index, dest, recv_slots, my_base, spilled, turned = prepared

    extent = (HOT + groups * MAIN + jnp.where(spilled, groups * spill, 0)) // CHUNK
    extent = extent.astype(jnp.int32).reshape(1)

    def gather_own(extra):
        own = gather_rows(index[:1], dest, extent, [hot_table, main, extra], parts, part_rows)
        return own, extra

    own_rows, extra = lax.cond(
        spilled,
        lambda: gather_own(exchange(MAIN, spill, ())[0]),
        lambda: gather_own(unused_rows(groups * spill, feat_cols, cold_table.dtype)),
    )
    sources = [hot_table, main, extra]
    own_rows, others = lax.optimization_barrier((own_rows, index[1:]))
    own_rows = send_round(own_rows)
    mean_rows = gather_rows(others, dest, extent, sources, parts, part_rows)
    mean_rows = send_round(mean_rows)
    send_rows, own_two = layer_one(
        me.reshape(1), my_base, own_rows, mean_rows, weights, groups, slots, own_part
    )
    send_rows = send_rows.reshape(groups * parts, slots, hidden_part)
    recv_rows = lax.all_to_all(send_rows, ("grp", "feat"), split_axis=0, concat_axis=0, tiled=True)
    recv_rows = recv_rows.reshape(groups * capacity, hidden_part)

    member = jnp.arange(targets, dtype=jnp.int32)[:, None] == recv_slots[None, :]
    total = jnp.dot(member.astype(jnp.bfloat16), recv_rows, preferred_element_type=jnp.float32)
    count = jnp.sum(member.astype(jnp.float32), axis=1)
    neigh_h = (total / jnp.maximum(count, 1.0)[:, None]).astype(jnp.bfloat16)
    partial_two = jnp.dot(neigh_h, turned, preferred_element_type=jnp.float32)
    holds = (jnp.arange(parts) == me)[:, None, None]
    partial_two = partial_two.reshape(parts, own_part, hidden) + jnp.where(holds, own_two[None], 0.0)
    partial_two = partial_two.reshape(targets, hidden)
    shared = send_round(jnp.split(partial_two, parts, axis=1))
    return (sum(shared[1:], shared[0]) + b2_bias).astype(jnp.bfloat16)


def solution(mesh):
    in_specs = (
        P(None, "feat"),
        P("grp", "feat"),
        P("grp", None, None),
        P("grp", None),
        P("grp"),
        P("grp", None),
        P("grp", None),
        P("grp"),
        P("feat", None),
        P("feat", None),
        P("feat"),
        P("feat", None),
        P("feat", None),
        P("feat"),
    )
    out_specs = P("grp", "feat")
    return jax.shard_map(
        per_device, mesh=mesh, in_specs=in_specs, out_specs=out_specs, check_vma=False
    )
```

```python
import functools

import jax
import jax.numpy as jnp
import numpy as np
from jax import lax
from jax.experimental import pallas as pl
from jax.experimental.pallas import tpu as pltpu
from jax.sharding import PartitionSpec as P


BLK = 128
LANES = 128
HOT = 16384
MAIN = 480
PREFIX_AT = 32
FLAG_AT = 64


def mark_kernel(refs, before, owners, extras, notes, look, acc):
    owner_rows = before.shape[0]
    groups = notes.shape[0]
    slot_count = owner_rows // groups
    acc[...] = jnp.zeros_like(acc)
    high = lax.broadcasted_iota(jnp.int32, (owner_rows, LANES), 0).astype(jnp.bfloat16)
    low = lax.broadcasted_iota(jnp.int32, (LANES, LANES), 0)
    low_half = low.astype(jnp.bfloat16)
    one, zero = jnp.bfloat16(1.0), jnp.bfloat16(0.0)

    def count(g, carry):
        tall, wide = [], []
        for j in range(2):
            cold = refs[pl.ds(2 * g + j, 1), :] - HOT
            tall.append(jnp.where(high == (cold >> 7).astype(jnp.bfloat16), one, zero))
            wide.append(jnp.where(low_half == (cold & 127).astype(jnp.bfloat16), one, zero))
        acc[...] += lax.dot_general(
            jnp.concatenate(tall, axis=1),
            jnp.concatenate(wide, axis=1),
            (((1,), (1,)), ((), ())),
            preferred_element_type=jnp.float32,
        )
        return carry

    lax.fori_loop(0, refs.shape[0] // 2, count, 0, unroll=11)
    needed = jnp.where(acc[...] > 0.0, 1.0, 0.0)
    upto = jnp.where(low <= lax.broadcasted_iota(jnp.int32, (LANES, LANES), 1), 1.0, 0.0)
    running = jnp.dot(
        needed.astype(jnp.bfloat16), upto.astype(jnp.bfloat16), preferred_element_type=jnp.float32
    )
    totals = jnp.dot(
        needed.astype(jnp.bfloat16),
        jnp.ones((LANES, LANES), jnp.bfloat16),
        preferred_element_type=jnp.float32,
    )
    earlier = jnp.dot(before[...], totals.astype(jnp.bfloat16), preferred_element_type=jnp.float32)
    local = jnp.where(needed > 0.0, running - 1.0, -1.0)
    place = jnp.where(needed > 0.0, earlier + running - 1.0, -1.0)
    spills = jnp.where(jnp.max(place) >= MAIN, 1, 0)
    place = place.astype(jnp.int32)
    lane = lax.broadcasted_iota(jnp.int32, (slot_count, LANES), 1)
    slot_lane = lane - PREFIX_AT == lax.broadcasted_iota(jnp.int32, (slot_count, LANES), 0)
    row_lane = lax.broadcasted_iota(jnp.int32, (1, LANES), 1)
    for o in range(groups):
        span = slice(o * slot_count, (o + 1) * slot_count)
        notes[o, 0:slot_count, :] = place[span]
        prefix = jnp.sum(jnp.where(slot_lane, earlier[span], 0.0), axis=0, keepdims=True)
        last = jnp.where(row_lane < PREFIX_AT, extras[o, 1:2, :], prefix.astype(jnp.int32))
        notes[o, slot_count : slot_count + 1, :] = extras[o, 0:1, :]
        notes[o, slot_count + 1 : slot_count + 2, :] = jnp.where(row_lane >= FLAG_AT, spills, last)
    across = jnp.transpose(earlier)[0:1]
    eighth = jnp.floor(across * 0.125)
    rest = jnp.zeros((5, owner_rows), jnp.float32)
    rows = [jnp.transpose(local), owners[0:1, :], eighth, across - 8.0 * eighth, rest]
    look[...] = jnp.concatenate(rows, axis=0).astype(jnp.bfloat16)


def mark_rows(refs, extras, slot_count, groups):
    rows = groups * slot_count
    at = np.arange(rows)
    before = (at[:, None] // slot_count == at[None, :] // slot_count) & (at[None, :] < at[:, None])
    before = jnp.asarray(before.astype(np.float32), jnp.bfloat16)
    owners = jnp.asarray(np.broadcast_to((at // slot_count)[None, :], (8, rows)), jnp.float32)
    return pl.pallas_call(
        mark_kernel,
        out_shape=(
            jax.ShapeDtypeStruct((groups, slot_count + 2, LANES), jnp.int32),
            jax.ShapeDtypeStruct((LANES + 8, rows), jnp.bfloat16),
        ),
        in_specs=[pl.BlockSpec(memory_space=pltpu.VMEM)] * 4,
        out_specs=(pl.BlockSpec(memory_space=pltpu.VMEM),) * 2,
        scratch_shapes=[pltpu.VMEM((rows, LANES), jnp.float32)],
        name="mark_rows",
    )(refs, before, owners, extras)


def remap_kernel(spill, groups, refs, look, *outs):
    owner_rows = look.shape[1]
    high = lax.broadcasted_iota(jnp.int32, (owner_rows, LANES), 0).astype(jnp.bfloat16)
    low = lax.broadcasted_iota(jnp.int32, (LANES, LANES), 0)
    one, zero = jnp.bfloat16(1.0), jnp.bfloat16(0.0)
    rows = outs[0].shape[0]
    table = look[...]
    for k, out in enumerate(outs):

        def lookup(g, carry, k=k, out=out):
            names = [refs[pl.ds(k * rows + 2 * g + j, 1), :] for j in range(2)]
            tall = [
                jnp.where(high == ((name - HOT) >> 7).astype(jnp.bfloat16), one, zero)
                for name in names
            ]
            found = jnp.dot(
                table, jnp.concatenate(tall, axis=1), preferred_element_type=jnp.float32
            )
            for j, name in enumerate(names):
                part = found[:, j * LANES : (j + 1) * LANES]
                local = jnp.where(low == ((name - HOT) & 127), part[:LANES], 0.0)
                local = jnp.sum(local, axis=0, keepdims=True)
                owner, eighth, unit = (part[LANES + n : LANES + n + 1] for n in range(3))
                place = 8.0 * eighth + unit + local
                cold = jnp.where(
                    place < MAIN,
                    HOT + owner * MAIN + place,
                    HOT + groups * MAIN + owner * spill + place - MAIN,
                ).astype(jnp.int32)
                out[pl.ds(2 * g + j, 1), :] = jnp.where(name < HOT, name, cold) * 2
            return carry

        lax.fori_loop(0, rows // 2, lookup, 0, unroll=11)


def remap(refs, look, nodes, spill, groups):
    count = refs.shape[0] * LANES // nodes
    outs = pl.pallas_call(
        functools.partial(remap_kernel, spill, groups),
        out_shape=[jax.ShapeDtypeStruct((nodes // LANES, LANES), jnp.int32)] * count,
        in_specs=[pl.BlockSpec(memory_space=pltpu.VMEM)] * 2,
        out_specs=[pl.BlockSpec(memory_space=pltpu.VMEM)] * count,
        name="remap",
    )(refs, look)
    return tuple(out.reshape(nodes) for out in outs)


TOGETHER = 4


def pack_kernel(first, slot_count, blocks, counts, prefix, need, cold, out, left, right):
    rows = out.shape[1]
    at = lax.broadcasted_iota(jnp.int32, (BLK, BLK), 0)
    for n in range(TOGETHER):
        r = pl.program_id(0) * TOGETHER + n
        for k in range(slot_count):
            begin = prefix[r * slot_count + k]
            place = need[n, k : k + 1, :] - begin
            place = jnp.where(counts[r] > k, place, -1)
            picks = jnp.where(at == place, 1.0, 0.0).astype(jnp.bfloat16)
            origin = pl.multiple_of(blocks[r * slot_count + k] * BLK, BLK)
            value = jnp.dot(picks, cold[pl.ds(origin, BLK), :], preferred_element_type=jnp.float32)
            left[n, pl.ds(begin, BLK), :] = value[:, :LANES]
            right[n, pl.ds(begin, BLK), :] = value[:, LANES:]
    for n in range(TOGETHER):
        out[n, :, :LANES] = left[n, first : first + rows, :].astype(out.dtype)
        out[n, :, LANES:] = right[n, first : first + rows, :].astype(out.dtype)


def pack_needed(blocks, counts, prefix, need, cold, first, rows):
    groups = counts.shape[0]
    cols = cold.shape[1]
    slot_count = blocks.shape[0] // groups
    return pl.pallas_call(
        functools.partial(pack_kernel, first, slot_count),
        grid=(groups // TOGETHER,),
        out_shape=jax.ShapeDtypeStruct((groups, rows, cols), cold.dtype),
        in_specs=[
            pl.BlockSpec(memory_space=pltpu.SMEM),
            pl.BlockSpec(memory_space=pltpu.SMEM),
            pl.BlockSpec(memory_space=pltpu.SMEM),
            pl.BlockSpec((TOGETHER,) + need.shape[1:], lambda r: (r, 0, 0)),
            pl.BlockSpec(memory_space=pltpu.VMEM),
        ],
        out_specs=pl.BlockSpec((TOGETHER, rows, cols), lambda r: (r, 0, 0)),
        scratch_shapes=[pltpu.VMEM((TOGETHER, slot_count * BLK + BLK, LANES), jnp.float32)] * 2,
        name="pack_needed",
    )(blocks, counts, prefix, need, cold)


def layer_one_kernel(parts, me, base, *refs):
    own, mean, weights = (refs[n * parts : (n + 1) * parts] for n in range(3))
    out, own_two, hidden, bias, product = refs[3 * parts :]
    half = own[0].shape[1]
    depth = 2 * half
    width = weights[0].shape[1]
    groups, _, slots, cols = out.shape
    own_part = own_two.shape[0]
    total_rows = own[0].shape[0]
    sources = [lax.rem(me[0] - step + parts, parts) for step in range(parts)]
    for source, weight in zip(sources, weights):
        tail = weight[depth + cols : depth + cols + 8, :cols].astype(jnp.float32)
        bias[:, pl.ds(pl.multiple_of(source * cols, cols), cols)] = (
            tail[0:1] + tail[1:2] + tail[2:3]
        )
    chunk = total_rows // 4
    for c in range(4):
        span = slice(c * chunk, (c + 1) * chunk)
        pre = jnp.broadcast_to(bias[...], (chunk, width))
        for self_x, neigh_x, weight in zip(own, mean, weights):
            pre = pre + jnp.dot(
                self_x[span, :], weight[0:half, :], preferred_element_type=jnp.float32
            )
            pre = pre + jnp.dot(
                neigh_x[span, :], weight[half:depth, :], preferred_element_type=jnp.float32
            )
        h1 = jnp.maximum(pre, 0.0).astype(jnp.bfloat16).astype(jnp.float32)
        for f in range(parts):
            hidden[f, span, :] = h1[:, f * cols : (f + 1) * cols]
    for f in range(parts):
        hidden[f, total_rows:, :] = jnp.zeros((hidden.shape[1] - total_rows, cols), jnp.float32)
    total = jnp.zeros((own_part, width), jnp.float32)
    for source, weight in zip(sources, weights):
        total = total + jnp.dot(
            hidden[source, 0:own_part, :].astype(jnp.bfloat16),
            weight[depth : depth + cols, :],
            preferred_element_type=jnp.float32,
        )
    product[...] = total
    for step in range(parts):
        column = pl.multiple_of(lax.rem(me[0] + step, parts) * cols, cols)
        own_two[:, step * cols : (step + 1) * cols] = product[:, pl.ds(column, cols)]

    def send(o, carry):
        for f in range(parts):
            out[o, f] = hidden[f, pl.ds(base[o], slots), :].astype(out.dtype)
        return carry

    lax.fori_loop(0, groups, send, 0, unroll=4)


def layer_one(me, base, own, mean, weights, groups, slots, own_part):
    parts = len(weights)
    total_rows = own[0].shape[0]
    width = weights[0].shape[1]
    cols = width // parts
    return pl.pallas_call(
        functools.partial(layer_one_kernel, parts),
        out_shape=(
            jax.ShapeDtypeStruct((groups, parts, slots, cols), jnp.bfloat16),
            jax.ShapeDtypeStruct((own_part, width), jnp.float32),
        ),
        in_specs=[pl.BlockSpec(memory_space=pltpu.SMEM)] * 2
        + [pl.BlockSpec(memory_space=pltpu.VMEM)] * (3 * parts),
        out_specs=(pl.BlockSpec(memory_space=pltpu.VMEM),) * 2,
        scratch_shapes=[
            pltpu.VMEM((parts, total_rows + slots, cols), jnp.float32),
            pltpu.VMEM((1, width), jnp.float32),
            pltpu.VMEM((own_part, width), jnp.float32),
        ],
        name="layer_one",
    )(me, base, *own, *mean, *weights)


CHUNK = 1024
DEPTH = 12


def gather_kernel(columns, source_count, dest, extent, *refs):
    index, refs = refs[:columns], refs[columns:]
    sources, refs = refs[:source_count], refs[source_count:]
    outs, (table, stage, acc, sems) = refs[:-4], refs[-4:]
    chunks = extent[0]
    nodes = dest.shape[0]

    def copy(c, slot):
        begin = 0
        for source in sources:
            length = source.shape[0] // CHUNK
            first = begin

            @pl.when((c >= first) & (c < first + length))
            def _():
                rows = pl.ds(pl.multiple_of((c - first) * CHUNK, CHUNK), CHUNK)
                pltpu.make_async_copy(source.at[rows], stage.at[slot], sems.at[slot]).start()

            begin += length

    for c in range(DEPTH):
        copy(c, c)

    def fill(i, carry):
        acc[pl.ds(pl.multiple_of(i * 8, 8), 8), :] = jnp.zeros((8, LANES), jnp.float32)
        return carry

    lax.fori_loop(0, acc.shape[0] // 8, fill, 0, unroll=8)

    def load(c, carry):
        slot = lax.rem(c, DEPTH)
        pltpu.make_async_copy(sources[0].at[pl.ds(0, CHUNK)], stage.at[slot], sems.at[slot]).wait()

        def widen(g, inner):
            value = stage[slot, pl.ds(pl.multiple_of(g * 16, 16), 16), :].astype(jnp.float32)
            row = pl.multiple_of(c * (2 * CHUNK) + g * 32, 32)
            table[pl.ds(row, 16, stride=2), :] = value[:, :LANES]
            table[pl.ds(row + 1, 16, stride=2), :] = value[:, LANES:]
            return inner

        lax.fori_loop(0, CHUNK // 16, widen, 0, unroll=8)

        @pl.when(c + DEPTH < chunks)
        def _():
            copy(c + DEPTH, slot)

        return carry

    lax.fori_loop(0, chunks, load, 0)

    def node(i, carry):
        rows = [table[pl.ds(pl.multiple_of(column[i], 2), 2), :] for column in index]
        while len(rows) > 1:
            rows = [a + b for a, b in zip(rows[::2], rows[1::2])] + rows[len(rows) // 2 * 2 :]
        acc[pl.ds(pl.multiple_of(dest[i], 2), 2), :] = rows[0]
        return carry

    lax.fori_loop(0, nodes, node, 0, unroll=16)

    for f, out in enumerate(outs):
        first = 2 * f * out.shape[0]

        def finish(g, carry, first=first, out=out):
            row = pl.multiple_of(first + g * 32, 32)
            halves = [acc[pl.ds(row + j, 16, stride=2), :] for j in range(2)]
            if columns > 1:
                halves = [half / columns for half in halves]
            out[pl.ds(pl.multiple_of(g * 16, 16), 16), :] = jnp.concatenate(halves, axis=1).astype(
                jnp.bfloat16
            )
            return carry

        lax.fori_loop(0, out.shape[0] // 16, finish, 0, unroll=2)


def gather_rows(index, dest, extent, sources, parts, rows):
    cols = sources[0].shape[1]
    table_rows = sum(source.shape[0] for source in sources)
    return pl.pallas_call(
        functools.partial(gather_kernel, len(index), len(sources)),
        out_shape=[jax.ShapeDtypeStruct((rows, cols), jnp.bfloat16)] * parts,
        in_specs=[pl.BlockSpec(memory_space=pltpu.SMEM)] * (2 + len(index))
        + [pl.BlockSpec(memory_space=pl.ANY)] * len(sources),
        out_specs=[pl.BlockSpec(memory_space=pltpu.VMEM)] * parts,
        scratch_shapes=[
            pltpu.VMEM((2 * table_rows, LANES), jnp.float32),
            pltpu.VMEM((DEPTH, CHUNK, cols), jnp.bfloat16),
            pltpu.VMEM((2 * parts * rows, LANES), jnp.float32),
            pltpu.SemaphoreType.DMA((DEPTH,)),
        ],
        compiler_params=pltpu.CompilerParams(vmem_limit_bytes=60 * 1024 * 1024),
    )(dest, extent, *index, *sources)


def unused_kernel(out):
    out[...] = jnp.zeros_like(out)


def unused_rows(rows, cols, dtype):
    return pl.pallas_call(
        unused_kernel,
        grid=(1,),
        out_shape=jax.ShapeDtypeStruct((rows, cols), dtype),
        out_specs=pl.BlockSpec((16, cols), lambda i: (0, 0)),
        name="unused_rows",
    )()


def send_round(chunks):
    parts = len(chunks)
    received = [chunks[0]]
    for step in range(1, parts):
        ring = [(s, (s + step) % parts) for s in range(parts)]
        received.append(lax.ppermute(chunks[step], "feat", ring))
    return received


def per_device(
    hot_table,
    cold_table,
    send_blocks,
    block_counts,
    self_ref,
    neigh_ref,
    route_owner,
    route_slot,
    w1_self,
    w1_neigh,
    b1_bias,
    w2_self,
    w2_neigh,
    b2_bias,
):
    groups = lax.axis_size("grp")
    parts = lax.axis_size("feat")
    me = lax.axis_index("feat")
    routed = route_slot.shape[0]
    nodes = self_ref.shape[0]
    targets = nodes - routed
    own_part = targets // parts
    hidden = w1_self.shape[1]
    hidden_part = b1_bias.shape[0]
    capacity = 2 * routed // groups
    slots = capacity // parts
    part_rows = own_part + (routed + (parts - 1) * groups) // parts
    part_rows = (part_rows + 15) // 16 * 16

    feat_cols = cold_table.shape[1]
    slot_count = send_blocks.shape[2]
    fetch_rows = slot_count * BLK
    refs = jnp.concatenate([self_ref, neigh_ref.T.reshape(-1)]).reshape(-1, LANES)

    coarse = lax.reduce_precision(b1_bias, 8, 7)
    middle = lax.reduce_precision(b1_bias - coarse, 8, 7)
    fine = b1_bias - coarse - middle
    bias_rows = jnp.stack([coarse, middle, fine]).astype(jnp.bfloat16)
    bias_rows = jnp.pad(bias_rows, ((0, 16 - 3), (0, hidden - hidden_part)))
    weight = jnp.concatenate([w1_self, w1_neigh, w2_self, bias_rows], axis=0)
    weights = [weight]
    for step in range(1, parts):
        ring = [(s, (s + step) % parts) for s in range(parts)]
        weights.append(lax.ppermute(weight, "feat", ring))

    owner = route_owner[:, 0]
    onehot = (owner[:, None] == jnp.arange(groups, dtype=jnp.int32)[None, :]).astype(jnp.int32)
    spans = routed // LANES
    upto = jnp.arange(LANES)[:, None] <= jnp.arange(LANES)[None, :]
    running = jnp.dot(
        onehot.T.astype(jnp.bfloat16).reshape(groups * spans, LANES),
        upto.astype(jnp.bfloat16),
        preferred_element_type=jnp.float32,
    ).reshape(groups, spans, LANES)
    span_totals = running[:, :, -1]
    before = jnp.arange(spans)[:, None] < jnp.arange(spans)[None, :]
    earlier = jnp.dot(
        span_totals.astype(jnp.bfloat16), before.astype(jnp.bfloat16), preferred_element_type=jnp.float32
    )
    ranks = (running + earlier[:, :, None]).astype(jnp.int32).reshape(groups, routed)
    position = jnp.sum((ranks - 1) * onehot.T, axis=0)
    quarter, depth = position % parts, position // parts
    totals = ranks[:, -1]
    held = (totals[None, :] - jnp.arange(parts)[:, None] + parts - 1) // parts
    base = jnp.cumsum(held, axis=1) - held + own_part
    owner_base = jnp.sum(onehot[:, :, None] * base.T[None, :, :], axis=1)
    mine = quarter[:, None] == jnp.arange(parts)[None, :]
    row_base = jnp.sum(jnp.where(mine, owner_base, 0), axis=1)
    routed_dest = (quarter - me + parts) % parts * part_rows + row_base + depth
    own = jnp.arange(targets, dtype=jnp.int32)
    own_dest = (own // own_part - me + parts) % parts * part_rows + own % own_part
    dest = jnp.concatenate([own_dest, routed_dest]) * 2

    column = quarter * slots + depth
    named = (column[:, None] == jnp.arange(capacity, dtype=jnp.int32)[None, :]).astype(jnp.bfloat16)
    send_slots = lax.dot_general(
        onehot.astype(jnp.bfloat16),
        named * (route_slot + 1).astype(jnp.bfloat16)[:, None],
        (((0,), (0,)), ((), ())),
        preferred_element_type=jnp.float32,
    )
    send_slots = send_slots.astype(jnp.int32) - 1
    extras = jnp.pad(send_slots, ((0, 0), (0, 2 * LANES - capacity))).reshape(groups, 2, LANES)
    notes, look = mark_rows(refs, extras, slot_count, groups)
    notes = lax.all_to_all(notes, "grp", split_axis=0, concat_axis=0, tiled=True)
    spill = fetch_rows - MAIN
    index = remap(refs, look, nodes, spill, groups)
    recv_slots = notes[:, slot_count:, :].reshape(groups, -1)[:, :capacity]
    recv_slots = recv_slots.reshape(groups * capacity)
    spilled = jnp.max(notes[:, slot_count + 1, FLAG_AT]) > 0
    prefix = notes[:, slot_count + 1, PREFIX_AT : PREFIX_AT + slot_count].reshape(-1)

    def exchange(first, rows, prepared):
        outgoing = pack_needed(
            send_blocks.reshape(-1),
            block_counts.reshape(-1),
            prefix,
            notes,
            cold_table,
            first,
            rows,
        )
        outgoing, prepared = lax.optimization_barrier((outgoing, prepared))
        fetched = lax.all_to_all(outgoing, "grp", split_axis=0, concat_axis=0, tiled=True)
        fetched, prepared = lax.optimization_barrier((fetched, prepared))
        return fetched.reshape(-1, feat_cols), prepared

    my_base = lax.dynamic_index_in_dim(base, me, 0, keepdims=False)

    turned = lax.dynamic_slice_in_dim(
        jnp.concatenate([w2_neigh, w2_neigh], axis=1), me * hidden_part, hidden, 1
    )
    prepared = (weights, index, dest, recv_slots, my_base, spilled, turned)
    main, prepared = exchange(0, MAIN, prepared)
    weights, index, dest, recv_slots, my_base, spilled, turned = prepared

    extent = (HOT + groups * MAIN + jnp.where(spilled, groups * spill, 0)) // CHUNK
    extent = extent.astype(jnp.int32).reshape(1)

    def gather_own(extra):
        own = gather_rows(index[:1], dest, extent, [hot_table, main, extra], parts, part_rows)
        return own, extra

    own_rows, extra = lax.cond(
        spilled,
        lambda: gather_own(exchange(MAIN, spill, ())[0]),
        lambda: gather_own(unused_rows(groups * spill, feat_cols, cold_table.dtype)),
    )
    sources = [hot_table, main, extra]
    own_rows, others = lax.optimization_barrier((own_rows, index[1:]))
    own_rows = send_round(own_rows)
    mean_rows = gather_rows(others, dest, extent, sources, parts, part_rows)
    mean_rows = send_round(mean_rows)
    send_rows, own_two = layer_one(
        me.reshape(1), my_base, own_rows, mean_rows, weights, groups, slots, own_part
    )
    send_rows = send_rows.reshape(groups * parts, slots, hidden_part)
    recv_rows = lax.all_to_all(send_rows, ("grp", "feat"), split_axis=0, concat_axis=0, tiled=True)
    recv_rows = recv_rows.reshape(groups * capacity, hidden_part)

    member = jnp.arange(targets, dtype=jnp.int32)[:, None] == recv_slots[None, :]
    total = jnp.dot(member.astype(jnp.bfloat16), recv_rows, preferred_element_type=jnp.float32)
    count = jnp.sum(member.astype(jnp.float32), axis=1)
    neigh_h = (total / jnp.maximum(count, 1.0)[:, None]).astype(jnp.bfloat16)
    partial_two = jnp.dot(neigh_h, turned, preferred_element_type=jnp.float32)
    holds = (jnp.arange(parts) == me)[:, None, None]
    partial_two = partial_two.reshape(parts, own_part, hidden) + jnp.where(holds, own_two[None], 0.0)
    partial_two = partial_two.reshape(targets, hidden)
    shared = send_round(jnp.split(partial_two, parts, axis=1))
    return (sum(shared[1:], shared[0]) + b2_bias).astype(jnp.bfloat16)


def solution(mesh):
    in_specs = (
        P(None, "feat"),
        P("grp", "feat"),
        P("grp", None, None),
        P("grp", None),
        P("grp"),
        P("grp", None),
        P("grp", None),
        P("grp"),
        P("feat", None),
        P("feat", None),
        P("feat"),
        P("feat", None),
        P("feat", None),
        P("feat"),
    )
    out_specs = P("grp", "feat")
    return jax.shard_map(
        per_device, mesh=mesh, in_specs=in_specs, out_specs=out_specs, check_vma=False
    )
```
